256 devices in a mesh: node: 4 (over z_lo), space: 64 (over y, z_hi, x, core).
Axes of the slice: x: 4, y: 4, z: 8 (z_hi: 2, z_lo: 4; z = z_hi * 4 + z_lo), core: 2. Of those that a mesh axis runs over, the one named last changes fastest.
Arguments:
- start_state: float32 [5, 4, 4, 4, 64, 1280], P(None, None, None, None, 'space'), may hold values from -1.5 to 14, as said below
- node_offset: float32 [4, 5, 4, 4, 4, 64, 1280], P('node', None, None, None, None, 'space'), may hold values from -0.6 to 0.6
Outputs:
- increments: float32 [4, 5, 4, 4, 4, 64, 1280], P('node', None, None, None, None, 'space')
The draws below stay inside these ranges and needn't reach their ends.
Inputs may be any that keep to these rules, and one draw needn't show every extreme that they name: `start_state`: conserved variables of a gas with gamma 1.4, density and pressure between 2 and 5 and every velocity component within 0.3 in magnitude, drawn independently at each node.
All inputs are finite; a program needn't handle non-finite values.
Results may differ from the reference program's by a relative error of at most 0.0001.
Values sent between devices are 32-bit elements; how exact they have to be, the bound alone decides.
A program may use at most 64 MiB of HBM per device.

```python
import math
import jax
import jax.numpy as jnp
import numpy as np
from jax import lax

EY = 16
EZ = 80
BASIS = 4
VARIABLES = 5
TIME_NODES = 4
ITERS = 2
NXE = 64
PLANE = 1280


def draw_start_state(key, part):
    subkeys = jax.random.split(key, 3)
    grid_shape = (4, 4, 4, NXE, PLANE)
    density = jax.random.uniform(subkeys[0], grid_shape, jnp.float32, 2.0, 4.0)
    pressure = jax.random.uniform(subkeys[2], grid_shape, jnp.float32, 2.0, 4.0)
    velocity = jax.random.uniform(subkeys[1], (3,) + grid_shape, jnp.float32, -0.3, 0.3)
    momenta = density * velocity
    energy = pressure / 0.4 + 0.5 * density * jnp.sum(velocity * velocity, axis=0)
    return jnp.concatenate([density[None], momenta, energy[None]], axis=0)


def shard_levels(rng, extent, cuts, smallest, top_value):
    gain = 1.0
    for axis_at, shards_of in cuts:
        steps = jax.random.uniform(jax.random.fold_in(jax.random.fold_in(rng, 6), axis_at), (shards_of,), jnp.float32, smallest / len(cuts), top_value / len(cuts))
        gain = gain * jnp.repeat(jnp.exp(steps), extent[axis_at] // shards_of).reshape((-1,) + (1,) * (len(extent) - 1 - axis_at))
    return gain


def gaussian(key, extent, spread, most, cuts=(), kind=jnp.bfloat16):
    gain = shard_levels(key, extent, cuts, -0.22, 0.18) if cuts else 1.0
    entries = jax.random.normal(key, extent, jnp.float32) * spread * gain
    return jnp.minimum(jnp.maximum(entries, -most), most).astype(kind)


def setup_inputs(seed: int = 0) -> dict:
    splits = jax.random.split(jax.random.key(seed), 3)
    start_state = draw_start_state(jax.random.fold_in(splits[2], 71), 0)
    node_offset = gaussian(splits[1], (TIME_NODES, VARIABLES, BASIS, BASIS, BASIS, NXE, PLANE), 0.15, 0.6, ((0, 4), (5, 64)), jnp.float32)
    return dict(start_state=start_state, node_offset=node_offset)


gamma_gas = 1.4
step_length = 0.01
inverse_weight = 6.0
highest = lax.Precision.HIGHEST
derivative_forms = ('ia,vabcxyz->vibcxyz', 'ib,vabcxyz->vaicxyz', 'ic,vabcxyz->vabixyz')

def lobatto_derivative():
    points = np.array([-1.0, -math.sqrt(0.2), math.sqrt(0.2), 1.0])
    barycentric = np.ones(4)
    for i in range(4):
        for k in range(4):
            if k != i:
                barycentric[i] = barycentric[i] / (points[i] - points[k])
    derivative = np.zeros((4, 4))
    for i in range(4):
        for j in range(4):
            if i != j:
                derivative[i, j] = barycentric[j] / barycentric[i] / (points[i] - points[j])
        derivative[i, i] = -np.sum(derivative[i])
    return derivative

def collocation_matrix():
    near_root = math.sqrt(3.0 / 7 - 2.0 / 7 * math.sqrt(1.2))
    far_root = math.sqrt(3.0 / 7 + 2.0 / 7 * math.sqrt(1.2))
    time_nodes = [(1.0 + value) / 2 for value in (-far_root, -near_root, near_root, far_root)]
    quad_table = np.zeros((4, 4))
    for j in range(4):
        coeffs = [1.0]
        for k in range(4):
            if k != j:
                scale = 1.0 / (time_nodes[j] - time_nodes[k])
                widened = [0.0] * (len(coeffs) + 1)
                for power in range(len(coeffs)):
                    widened[power + 1] = widened[power + 1] + coeffs[power] * scale
                    widened[power] = widened[power] - time_nodes[k] * coeffs[power] * scale
                coeffs = widened
        for m in range(4):
            total = 0.0
            for power in range(len(coeffs)):
                total = total + coeffs[power] * time_nodes[m] ** (power + 1) / (power + 1)
            quad_table[m, j] = total
    return quad_table

def physical_flux(state, direction):
    density = state[0]
    momenta = state[1:4]
    energy = state[4]
    velocity = momenta / density
    pressure = (gamma_gas - 1.0) * (energy - 0.5 * lax.optimization_barrier(jnp.sum(momenta * velocity, axis=0)))
    normal_speed = velocity[direction]
    columns = [momenta[direction]]
    for component in range(3):
        entry = momenta[component] * normal_speed
        if component == direction:
            entry = entry + pressure
        columns.append(entry)
    columns.append((energy + pressure) * normal_speed)
    return (jnp.stack(columns), jnp.abs(normal_speed) + jnp.sqrt(gamma_gas * pressure / density))

def face_flux(left_state, right_state, direction):
    left_flux, left_wave = physical_flux(left_state, direction)
    right_flux, right_wave = physical_flux(right_state, direction)
    wave_speed = jnp.maximum(left_wave, right_wave)
    return 0.5 * (left_flux + right_flux) - 0.5 * wave_speed * (right_state - left_state)

def edge_slice(array, dim, first):
    return lax.slice_in_dim(array, first, first + 1, axis=dim)

def with_surface(first_term, last_term, dim):
    filler = jnp.zeros_like(first_term)
    return jnp.concatenate([first_term, filler, filler, last_term], axis=dim)

def element_rate(state):
    cube = state.reshape(state.shape[:5] + (EY, EZ))
    derivative = jnp.asarray(lobatto_derivative(), jnp.float32)
    total_rate = jnp.zeros_like(cube)
    for direction in range(3):
        flux, wave_unused = physical_flux(cube, direction)
        total_rate = total_rate - jnp.einsum(derivative_forms[direction], derivative, flux, precision=highest)
        node_dim = 1 + direction
        elem_dim = 4 + direction
        own_first = edge_slice(cube, node_dim, 0)
        own_last = edge_slice(cube, node_dim, 3)
        right_faces = face_flux(own_last, jnp.roll(own_first, -1, axis=elem_dim), direction)
        left_faces = jnp.roll(right_faces, 1, axis=elem_dim)
        flux_first = edge_slice(flux, node_dim, 0)
        flux_last = edge_slice(flux, node_dim, 3)
        total_rate = total_rate + inverse_weight * with_surface(left_faces - flux_first, flux_last - right_faces, node_dim)
    return total_rate.reshape(state.shape)

def reference(start_state, node_offset):
    quad_table = jnp.asarray(collocation_matrix(), jnp.float32)
    states = [start_state + node_offset[position] for position in range(4)]
    results = []
    for iteration in range(ITERS):
        rates = [element_rate(current) for current in states]
        results = []
        for target in range(4):
            running = quad_table[target, 0] * rates[0]
            for source in range(1, 4):
                running = running + quad_table[target, source] * rates[source]
            results.append(step_length * running)
        states = [start_state + change for change in results]
    return jnp.stack(results)
```

```python
import functools
import math

import jax
import jax.numpy as jnp
import numpy as np
from jax import lax
from jax.experimental import pallas as pl
from jax.experimental.pallas import tpu as pltpu
from jax.sharding import PartitionSpec as P

MESH = pl.DeviceIdType.MESH
TILES = 10
GAS = 1.4
STEP = 0.01


def lobatto_derivative():
    points = np.array([-1.0, -math.sqrt(0.2), math.sqrt(0.2), 1.0])
    barycentric = np.ones(4)
    for i in range(4):
        for k in range(4):
            if k != i:
                barycentric[i] = barycentric[i] / (points[i] - points[k])
    derivative = np.zeros((4, 4))
    for i in range(4):
        for j in range(4):
            if i != j:
                derivative[i, j] = barycentric[j] / barycentric[i] / (points[i] - points[j])
        derivative[i, i] = -np.sum(derivative[i])
    return derivative


def collocation_matrix():
    near_root = math.sqrt(3.0 / 7 - 2.0 / 7 * math.sqrt(1.2))
    far_root = math.sqrt(3.0 / 7 + 2.0 / 7 * math.sqrt(1.2))
    time_nodes = [(1.0 + value) / 2 for value in (-far_root, -near_root, near_root, far_root)]
    quad_table = np.zeros((4, 4))
    for j in range(4):
        coeffs = [1.0]
        for k in range(4):
            if k != j:
                scale = 1.0 / (time_nodes[j] - time_nodes[k])
                widened = [0.0] * (len(coeffs) + 1)
                for power in range(len(coeffs)):
                    widened[power + 1] = widened[power + 1] + coeffs[power] * scale
                    widened[power] = widened[power] - time_nodes[k] * coeffs[power] * scale
                coeffs = widened
        for m in range(4):
            total = 0.0
            for power in range(len(coeffs)):
                total = total + coeffs[power] * time_nodes[m] ** (power + 1) / (power + 1)
            quad_table[m, j] = total
    return quad_table


D = [[float(value) for value in row] for row in lobatto_derivative()]
Q = [[float(STEP * value) for value in row] for row in collocation_matrix()]


def lanes():
    return lax.broadcasted_iota(jnp.int32, (8, 128), 1)


def upper_half():
    return lax.broadcasted_iota(jnp.int32, (8, 128), 0) < 4


def swap(value):
    return pltpu.roll(value, 4, 0)


def turn(value, shift):
    return pltpu.roll(value, shift, 1)


def primitives(state, direction):
    inverse = 1.0 / state[0]
    speeds = [state[1 + k] * inverse for k in range(3)]
    kinetic = state[1] * speeds[0] + state[2] * speeds[1] + state[3] * speeds[2]
    pressure = (GAS - 1.0) * (state[4] - 0.5 * kinetic)
    return inverse, speeds[direction], pressure


def fluxes(state, speed, pressure, direction):
    columns = [state[1 + direction]]
    for k in range(3):
        entry = state[1 + k] * speed
        columns.append(entry + pressure if k == direction else entry)
    columns.append((state[4] + pressure) * speed)
    return columns


def wave(inverse, speed, pressure):
    return jnp.abs(speed) + jnp.sqrt(GAS * pressure * inverse)


def lift(own, own_flux, own_wave, other, direction, sign):
    inverse, speed, pressure = primitives(other, direction)
    other_flux = fluxes(other, speed, pressure, direction)
    top = jnp.maximum(own_wave, wave(inverse, speed, pressure))
    return [
        3.0 * (sign * (other_flux[v] - own_flux[v]) + top * (other[v] - own[v])) for v in range(5)
    ]


def derivative(values):
    out = []
    for i in range(4):
        row = []
        for v in range(5):
            total = None
            for j in range(4):
                if abs(D[i][j]) > 1e-12:
                    term = (-D[i][j]) * values[j][v]
                    total = term if total is None else total + term
            row.append(total)
        out.append(row)
    return out


def strided(ref, at, v, pair, c):
    return ref[at, v, pl.ds(32 * pair + c, 8, 4), :]


def rows(ref, at, v, start):
    return ref[at, v, pl.ds(start, 8), :]


def pass_z(u, at, before, after, out, to, tile):
    lane = lanes()
    base = lax.rem(48 * tile, 80)
    place = lane + base
    first = (place == 0) | (place == 80) | (place == 160)
    last = (place == 79) | (place == 159)
    for pair in range(2):
        state = [[strided(u, at, v, pair, c) for v in range(5)] for c in range(4)]
        prims = [primitives(state[c], 2) for c in range(4)]
        flux = [fluxes(state[c], prims[c][1], prims[c][2], 2) for c in range(4)]
        rate = derivative(flux)
        left = []
        right = []
        for v in range(5):
            back = strided(u, before, v, pair, 3)
            ahead = strided(u, after, v, pair, 3)
            near = turn(jnp.where(lane == 127, back, state[3][v]), 1)
            far = turn(jnp.where(lane >= 79, state[3][v], ahead), 49)
            left.append(jnp.where(first, far, near))
            back = strided(u, before, v, pair, 0)
            ahead = strided(u, after, v, pair, 0)
            near = turn(jnp.where(lane == 0, ahead, state[0][v]), 127)
            far = turn(jnp.where(lane >= 49, back, state[0][v]), 79)
            right.append(jnp.where(last, far, near))
        low = lift(state[0], flux[0], wave(*prims[0]), left, 2, 1.0)
        high = lift(state[3], flux[3], wave(*prims[3]), right, 2, -1.0)
        for v in range(5):
            for c in range(4):
                value = rate[c][v]
                if c == 0:
                    value = value + low[v]
                if c == 3:
                    value = value + high[v]
                out[to, v, pl.ds(32 * pair + c, 8, 4), :] = value


def pass_y(u, at, before, after, out, to):
    lane = lanes()
    half = upper_half()
    sign = jnp.where(half, 1.0, -1.0).astype(jnp.float32)

    def two(x, y):
        return jnp.where(half, jnp.float32(-x), jnp.float32(-y))

    mix_low = [two(D[0][0], D[1][1]), two(D[0][1], D[1][0]), two(D[0][2], D[1][3]), two(D[0][3], D[1][2])]
    mix_high = [two(D[2][0], D[3][1]), two(D[2][1], D[3][0]), two(D[2][2], D[3][3]), two(D[2][3], D[3][2])]
    for a in range(4):
        low = [rows(u, at, v, 16 * a) for v in range(5)]
        high = [rows(u, at, v, 16 * a + 8) for v in range(5)]
        prim_low = primitives(low, 1)
        prim_high = primitives(high, 1)
        flux_low = fluxes(low, prim_low[1], prim_low[2], 1)
        flux_high = fluxes(high, prim_high[1], prim_high[2], 1)
        own = [jnp.where(half, low[v], high[v]) for v in range(5)]
        own_flux = [jnp.where(half, flux_low[v], flux_high[v]) for v in range(5)]
        own_wave = wave(*[jnp.where(half, x, y) for x, y in zip(prim_low, prim_high)])
        other = []
        for v in range(5):
            back = rows(u, before, v, 16 * a + 8)
            ahead = rows(u, after, v, 16 * a)
            down = turn(jnp.where(lane >= 48, back, high[v]), 80)
            up = turn(jnp.where(lane >= 80, low[v], ahead), 48)
            other.append(swap(jnp.where(half, up, down)))
        face = lift(own, own_flux, own_wave, other, 1, sign)
        for v in range(5):
            parts = [flux_low[v], swap(flux_low[v]), flux_high[v], swap(flux_high[v])]
            sum_low = jnp.where(half, face[v], 0.0)
            sum_high = jnp.where(half, 0.0, face[v])
            for k in range(4):
                sum_low = sum_low + mix_low[k] * parts[k]
                sum_high = sum_high + mix_high[k] * parts[k]
            out[to, v, pl.ds(16 * a, 8), :] += sum_low
            out[to, v, pl.ds(16 * a + 8, 8), :] += sum_high


def pass_x(u, at, out, to):
    for h in range(2):
        state = [[rows(u, at, v, 16 * a + 8 * h) for v in range(5)] for a in range(4)]
        flux = []
        for a in range(4):
            _, speed, pressure = primitives(state[a], 0)
            flux.append(fluxes(state[a], speed, pressure, 0))
        rate = derivative(flux)
        for a in range(4):
            for v in range(5):
                out[to, v, pl.ds(16 * a + 8 * h, 8), :] += rate[a][v]


def faces_x(u, at, lower, low_at, upper, up_at, out, to):
    for h in range(2):
        for a, other, sign in ((0, lower, 1.0), (3, upper, -1.0)):
            own = [rows(u, at, v, 16 * a + 8 * h) for v in range(5)]
            inverse, speed, pressure = primitives(own, 0)
            own_flux = fluxes(own, speed, pressure, 0)
            trace = [other(v, h) for v in range(5)]
            face = lift(own, own_flux, wave(inverse, speed, pressure), trace, 0, sign)
            for v in range(5):
                out[to, v, pl.ds(16 * a + 8 * h, 8), :] += face[v]


def inner_rate(u, at, before, after, out, to, tile):
    pass_z(u, at, before, after, out, to, tile)
    pass_y(u, at, before, after, out, to)
    pass_x(u, at, out, to)


def pack(ref, at, side, tile):
    lane = lanes()
    half = upper_half()
    packed = []
    for v in range(5):
        for pair in range(2):
            c0 = strided(ref, at, v, pair, 0)
            c3 = strided(ref, at, v, pair, 3)
            if side == 0:
                one = rows(ref, at, v, 32 * pair + 8)
                two = rows(ref, at, v, 32 * pair + 24)
                main = jnp.where(half, swap(one), two)
                main = jnp.where(lane == 0, turn(c0, 8 + 8 * tile), main)
                main = jnp.where(lane == 1, turn(c3, 2), main)
            else:
                one = rows(ref, at, v, 32 * pair)
                two = rows(ref, at, v, 32 * pair + 16)
                main = jnp.where(half, one, swap(two))
                main = jnp.where(lane == 127, turn(c0, 127), main)
                main = jnp.where(lane == 126, turn(c3, 47 + 8 * tile), main)
            packed.append(main)
    return packed


def unpack(packed, ref, at, side):
    for v in range(5):
        for pair in range(2):
            block = packed[2 * v + pair]
            at0, at3 = (0, 1) if side == 0 else (127, 126)
            c0 = jnp.broadcast_to(block[:, at0 : at0 + 1], (8, 128))
            c3 = jnp.broadcast_to(block[:, at3 : at3 + 1], (8, 128))
            ref[at, v, pl.ds(32 * pair, 8, 4), :] = c0
            ref[at, v, pl.ds(32 * pair + 3, 8, 4), :] = c3
            shift = 12 if side == 0 else 0
            ref[at, v, pl.ds(32 * pair + shift, 4), :] = block[0:4]
            ref[at, v, pl.ds(32 * pair + 16 + shift, 4), :] = block[4:8]


def tile_before(q):
    return 3 * q - 2 + 11 * ((3 - q) // 3)


def tile_after(q):
    return 3 * q + 2 - 11 * (q // 3)


def kernel(
    start_hbm,
    offset_hbm,
    out_hbm,
    start,
    u0,
    x_low,
    x_high,
    rate,
    halo_send,
    landed,
    halo,
    u1,
    x_low2,
    x_high2,
    rate2,
    give,
    load_sem,
    x_send,
    x_recv,
    mid_send,
    mid_recv,
    end_send,
    end_recv,
    halo_ssem,
    halo_rsem,
    own_sem,
    own_halo_sem,
    x_send2,
    x_recv2,
    give_send,
    give_recv,
    give_own,
):
    m = lax.axis_index("node")
    s = lax.axis_index("space")
    hi = (s // 8) % 2
    q = m + hi * (3 - 2 * m)
    up = (s + 1) % 64
    down = (s + 63) % 64
    hi_up = (up // 8) % 2
    hi_down = (down // 8) % 2
    q_up = q + hi_up * (3 - 2 * q)
    q_down = q + hi_down * (3 - 2 * q)
    slot_from = (3 - q) // 3
    slot_to = 3 - q // 3
    first_tile = 3 * q - 1

    def loads(t):
        return (
            pltpu.make_async_copy(start_hbm.at[:, :, t, 0, :], start.at[t], load_sem.at[0, t]),
            pltpu.make_async_copy(offset_hbm.at[:, :, t, 0, :], u0.at[t], load_sem.at[1, t]),
        )

    def begin(t, carry):
        one, two = loads(t)
        one.start()
        two.start()
        return carry

    lax.fori_loop(0, TILES, begin, 0)

    barrier = pltpu.get_barrier_semaphore()
    for k in range(1, 4):
        pl.semaphore_signal(barrier, inc=1, device_id={"node": (m + k) % 4}, device_id_type=MESH)
    pl.semaphore_signal(barrier, inc=1, device_id={"space": up}, device_id_type=MESH)
    pl.semaphore_signal(barrier, inc=1, device_id={"space": down}, device_id_type=MESH)
    pl.semaphore_signal(barrier, inc=1, device_id={"node": q_up, "space": up}, device_id_type=MESH)
    pl.semaphore_signal(barrier, inc=1, device_id={"node": q_down, "space": down}, device_id_type=MESH)
    pl.semaphore_wait(barrier, 7)

    def x_copies(t):
        return (
            pltpu.make_async_remote_copy(
                src_ref=u0.at[t, :, pl.ds(48, 16)],
                dst_ref=x_low.at[t],
                send_sem=x_send.at[0, t],
                recv_sem=x_recv.at[0, t],
                device_id={"space": up},
                device_id_type=MESH,
            ),
            pltpu.make_async_remote_copy(
                src_ref=u0.at[t, :, pl.ds(0, 16)],
                dst_ref=x_high.at[t],
                send_sem=x_send.at[1, t],
                recv_sem=x_recv.at[1, t],
                device_id={"space": down},
                device_id_type=MESH,
            ),
        )

    def guess(t, carry):
        one, two = loads(t)
        one.wait()
        two.wait()
        for v in range(5):
            u0[t, v] = u0[t, v] + start[t, v]
        one, two = x_copies(t)
        one.start()
        two.start()
        return carry

    lax.fori_loop(0, TILES, guess, 0)

    def owner(t):
        d = (t + 1) // 3
        return d, d + hi * (3 - 2 * d)

    def mid_copy(t):
        d, place = owner(t)
        return pltpu.make_async_remote_copy(
            src_ref=rate.at[t, :, pl.ds(16, 32)],
            dst_ref=landed.at[m, t - 3 * d + 1, :, pl.ds(16, 32)],
            send_sem=mid_send.at[t],
            recv_sem=mid_recv.at[m, t - 3 * d + 1],
            device_id={"node": place},
            device_id_type=MESH,
        )

    def end_copies(t):
        d, place = owner(t)
        return [
            pltpu.make_async_remote_copy(
                src_ref=rate.at[t, :, pl.ds(48 * k, 16)],
                dst_ref=landed.at[m, t - 3 * d + 1, :, pl.ds(48 * k, 16)],
                send_sem=end_send.at[k, t],
                recv_sem=end_recv.at[k, m, t - 3 * d + 1],
                device_id={"node": place},
                device_id_type=MESH,
            )
            for k in range(2)
        ]

    def own_copy(slot):
        return pltpu.make_async_copy(
            rate.at[first_tile + slot], landed.at[m, slot], own_sem.at[slot]
        )

    def inside(t, carry):
        inner_rate(u0, t, (t + 9) % 10, (t + 1) % 10, rate, t, t)
        d, place = owner(t)

        @pl.when(d != q)
        def _():
            mid_copy(t).start()

        return carry

    lax.fori_loop(0, TILES, inside, 0)

    def edges(t, carry):
        one, two = x_copies(t)
        one.wait_recv()
        two.wait_recv()
        faces_x(
            u0,
            t,
            lambda v, h: x_low[t, v, pl.ds(8 * h, 8), :],
            t,
            lambda v, h: x_high[t, v, pl.ds(8 * h, 8), :],
            t,
            rate,
            t,
        )
        d, place = owner(t)

        @pl.when(d != q)
        def _():
            for copy in end_copies(t):
                copy.start()

        @pl.when(d == q)
        def _():
            own_copy(t - first_tile).start()

        return carry

    lax.fori_loop(0, TILES, edges, 0)

    def halo_copies(d):
        place = d + hi * (3 - 2 * d)
        return [
            pltpu.make_async_remote_copy(
                src_ref=halo_send.at[d, side],
                dst_ref=halo.at[m, side],
                send_sem=halo_ssem.at[d, side],
                recv_sem=halo_rsem.at[m, side],
                device_id={"node": place},
                device_id_type=MESH,
            )
            for side in range(2)
        ]

    def own_halo(side):
        return pltpu.make_async_copy(halo_send.at[q, side], halo.at[m, side], own_halo_sem.at[side])

    def borders(d, carry):
        for side, tile in ((0, tile_before(d)), (1, tile_after(d))):
            for k, block in enumerate(pack(rate, tile, side, tile)):
                halo_send[d, side, pl.ds(8 * k, 8), :] = block

        @pl.when(d != q)
        def _():
            for copy in halo_copies(d):
                copy.start()

        @pl.when(d == q)
        def _():
            for side in range(2):
                own_halo(side).start()

        return carry

    lax.fori_loop(0, 4, borders, 0)

    def arrive(j, carry):
        @pl.when(j != m)
        def _():
            def each(slot, inner):
                whole = landed.at[j, slot]
                for part, sem in (
                    (whole.at[:, pl.ds(16, 32)], mid_recv.at[j, slot]),
                    (whole.at[:, pl.ds(0, 16)], end_recv.at[0, j, slot]),
                    (whole.at[:, pl.ds(48, 16)], end_recv.at[1, j, slot]),
                ):
                    pltpu.make_async_remote_copy(
                        src_ref=part,
                        dst_ref=part,
                        send_sem=mid_send.at[0],
                        recv_sem=sem,
                        device_id={"node": (m + 1) % 4},
                        device_id_type=MESH,
                    ).wait_recv()
                return inner

            lax.fori_loop(slot_from, slot_to, each, 0)
            for side in range(2):
                pltpu.make_async_remote_copy(
                    src_ref=halo.at[j, side],
                    dst_ref=halo.at[j, side],
                    send_sem=mid_send.at[0],
                    recv_sem=halo_rsem.at[j, side],
                    device_id={"node": (m + 1) % 4},
                    device_id_type=MESH,
                ).wait_recv()

        @pl.when(j == m)
        def _():
            def each(slot, inner):
                own_copy(slot).wait()
                return inner

            lax.fori_loop(slot_from, slot_to, each, 0)
            for side in range(2):
                own_halo(side).wait()

        return carry

    lax.fori_loop(0, 4, arrive, 0)

    def x_copies2(slot):
        return (
            pltpu.make_async_remote_copy(
                src_ref=u1.at[:, slot + 1, :, pl.ds(48, 16)],
                dst_ref=x_low2.at[slot],
                send_sem=x_send2.at[0, slot],
                recv_sem=x_recv2.at[0, slot],
                device_id={"node": q_up, "space": up},
                device_id_type=MESH,
            ),
            pltpu.make_async_remote_copy(
                src_ref=u1.at[:, slot + 1, :, pl.ds(0, 16)],
                dst_ref=x_high2.at[slot],
                send_sem=x_send2.at[1, slot],
                recv_sem=x_recv2.at[1, slot],
                device_id={"node": q_down, "space": down},
                device_id_type=MESH,
            ),
        )

    def advance(slot, carry):
        def each(part, inner):
            v = part // 8
            at = pl.multiple_of((part % 8) * 8, 8)
            held = [landed[j, slot, v, pl.ds(at, 8), :] for j in range(4)]
            base = start[first_tile + slot, v, pl.ds(at, 8), :]
            for k in range(4):
                total = Q[k][0] * held[0]
                for j in range(1, 4):
                    total = total + Q[k][j] * held[j]
                u1[k, slot + 1, v, pl.ds(at, 8), :] = base + total
            return inner

        lax.fori_loop(0, 40, each, 0)
        one, two = x_copies2(slot)
        one.start()
        two.start()
        return carry

    lax.fori_loop(slot_from, slot_to, advance, 0)

    for side, tile, at in ((0, tile_before(q), slot_from), (1, tile_after(q), slot_to + 1)):
        base = pack(start, tile, side, tile)
        held = [[halo[j, side, pl.ds(8 * k, 8), :] for k in range(10)] for j in range(4)]
        for node in range(4):
            blocks = []
            for k in range(10):
                total = Q[node][0] * held[0][k]
                for j in range(1, 4):
                    total = total + Q[node][j] * held[j][k]
                blocks.append(base[k] + total)
            unpack(blocks, u1.at[node], at, side)

    def inside2(slot, carry):
        def each(node, inner):
            inner_rate(
                u1.at[node],
                slot + 1,
                slot,
                slot + 2,
                rate2.at[node],
                slot,
                first_tile + slot,
            )
            return inner

        lax.fori_loop(0, 4, each, 0)
        return carry

    lax.fori_loop(slot_from, slot_to, inside2, 0)

    def give_copy(node, slot):
        return pltpu.make_async_remote_copy(
            src_ref=give.at[node, slot],
            dst_ref=out_hbm.at[:, :, first_tile + slot, 0, :],
            send_sem=give_send.at[node, slot],
            recv_sem=give_recv.at[first_tile + slot],
            device_id={"node": node},
            device_id_type=MESH,
        )

    def give_here(slot):
        return pltpu.make_async_copy(
            give.at[m, slot], out_hbm.at[:, :, first_tile + slot, 0, :], give_own.at[slot]
        )

    def edges2(slot, carry):
        one, two = x_copies2(slot)
        one.wait_recv()
        two.wait_recv()

        def each(node, inner):
            faces_x(
                u1.at[node],
                slot + 1,
                lambda v, h: x_low2[slot, node, v, pl.ds(8 * h, 8), :],
                slot,
                lambda v, h: x_high2[slot, node, v, pl.ds(8 * h, 8), :],
                slot,
                rate2.at[node],
                slot,
            )
            return inner

        lax.fori_loop(0, 4, each, 0)

        def gather(part, inner):
            v = part // 8
            at = pl.multiple_of((part % 8) * 8, 8)
            held = [rate2[j, slot, v, pl.ds(at, 8), :] for j in range(4)]
            for k in range(4):
                total = Q[k][0] * held[0]
                for j in range(1, 4):
                    total = total + Q[k][j] * held[j]
                give[k, slot, v, pl.ds(at, 8), :] = total
            return inner

        lax.fori_loop(0, 40, gather, 0)

        def send(node, inner):
            @pl.when(node != m)
            def _():
                give_copy(node, slot).start()

            @pl.when(node == m)
            def _():
                give_here(slot).start()

            return inner

        lax.fori_loop(0, 4, send, 0)
        return carry

    lax.fori_loop(slot_from, slot_to, edges2, 0)

    def drain(t, carry):
        one, two = x_copies(t)
        one.wait_send()
        two.wait_send()
        d, place = owner(t)

        @pl.when(d != q)
        def _():
            mid_copy(t).wait_send()
            for copy in end_copies(t):
                copy.wait_send()
            here = out_hbm.at[:, :, t, 0, :]
            pltpu.make_async_remote_copy(
                src_ref=here,
                dst_ref=here,
                send_sem=mid_send.at[0],
                recv_sem=give_recv.at[t],
                device_id={"node": (m + 1) % 4},
                device_id_type=MESH,
            ).wait_recv()

        return carry

    lax.fori_loop(0, TILES, drain, 0)

    def drain_nodes(d, carry):
        @pl.when(d != q)
        def _():
            for copy in halo_copies(d):
                copy.wait_send()

        return carry

    lax.fori_loop(0, 4, drain_nodes, 0)

    def drain_slots(slot, carry):
        one, two = x_copies2(slot)
        one.wait_send()
        two.wait_send()
        give_here(slot).wait()

        def each(node, inner):
            @pl.when(node != m)
            def _():
                give_copy(node, slot).wait_send()

            return inner

        lax.fori_loop(0, 4, each, 0)
        return carry

    lax.fori_loop(slot_from, slot_to, drain_slots, 0)


def body(start_state, node_offset):
    flat = (5, 64, TILES, 1, 128)
    vmem = lambda *shape: pltpu.VMEM(shape, jnp.float32)
    dma = lambda *shape: pltpu.SemaphoreType.DMA(shape)
    out = pl.pallas_call(
        kernel,
        out_shape=jax.ShapeDtypeStruct(flat, jnp.float32),
        in_specs=[pl.BlockSpec(memory_space=pltpu.HBM)] * 2,
        out_specs=pl.BlockSpec(memory_space=pltpu.HBM),
        scratch_shapes=[
            vmem(10, 5, 64, 128),
            vmem(10, 5, 64, 128),
            vmem(10, 5, 16, 128),
            vmem(10, 5, 16, 128),
            vmem(10, 5, 64, 128),
            vmem(4, 2, 80, 128),
            vmem(4, 3, 5, 64, 128),
            vmem(4, 2, 80, 128),
            vmem(4, 5, 5, 64, 128),
            vmem(3, 4, 5, 16, 128),
            vmem(3, 4, 5, 16, 128),
            vmem(4, 3, 5, 64, 128),
            vmem(4, 3, 5, 64, 128),
            dma(2, 10),
            dma(2, 10),
            dma(2, 10),
            dma(10),
            dma(4, 3),
            dma(2, 10),
            dma(2, 4, 3),
            dma(4, 2),
            dma(4, 2),
            dma(3),
            dma(2),
            dma(2, 3),
            dma(2, 3),
            dma(4, 3),
            dma(10),
            dma(3),
        ],
        compiler_params=pltpu.CompilerParams(
            collective_id=0, has_side_effects=True, vmem_limit_bytes=56 << 20
        ),
    )(start_state.reshape(flat), node_offset.reshape(flat))
    return out.reshape((1,) + start_state.shape)


def solution(mesh):
    return jax.shard_map(
        body,
        mesh=mesh,
        in_specs=(
            P(None, None, None, None, "space", None),
            P("node", None, None, None, None, "space", None),
        ),
        out_specs=P("node", None, None, None, None, "space", None),
        check_vma=False,
    )
```

```python
import functools
import math

import jax
import jax.numpy as jnp
import numpy as np
from jax import lax
from jax.experimental import pallas as pl
from jax.experimental.pallas import tpu as pltpu
from jax.sharding import PartitionSpec as P

MESH = pl.DeviceIdType.MESH
TILES = 10
GAS = 1.4
STEP = 0.01


def lobatto_derivative():
    points = np.array([-1.0, -math.sqrt(0.2), math.sqrt(0.2), 1.0])
    barycentric = np.ones(4)
    for i in range(4):
        for k in range(4):
            if k != i:
                barycentric[i] = barycentric[i] / (points[i] - points[k])
    derivative = np.zeros((4, 4))
    for i in range(4):
        for j in range(4):
            if i != j:
                derivative[i, j] = barycentric[j] / barycentric[i] / (points[i] - points[j])
        derivative[i, i] = -np.sum(derivative[i])
    return derivative


def collocation_matrix():
    near_root = math.sqrt(3.0 / 7 - 2.0 / 7 * math.sqrt(1.2))
    far_root = math.sqrt(3.0 / 7 + 2.0 / 7 * math.sqrt(1.2))
    time_nodes = [(1.0 + value) / 2 for value in (-far_root, -near_root, near_root, far_root)]
    quad_table = np.zeros((4, 4))
    for j in range(4):
        coeffs = [1.0]
        for k in range(4):
            if k != j:
                scale = 1.0 / (time_nodes[j] - time_nodes[k])
                widened = [0.0] * (len(coeffs) + 1)
                for power in range(len(coeffs)):
                    widened[power + 1] = widened[power + 1] + coeffs[power] * scale
                    widened[power] = widened[power] - time_nodes[k] * coeffs[power] * scale
                coeffs = widened
        for m in range(4):
            total = 0.0
            for power in range(len(coeffs)):
                total = total + coeffs[power] * time_nodes[m] ** (power + 1) / (power + 1)
            quad_table[m, j] = total
    return quad_table


D = [[float(value) for value in row] for row in lobatto_derivative()]
Q = [[float(STEP * value) for value in row] for row in collocation_matrix()]


def lanes():
    return lax.broadcasted_iota(jnp.int32, (8, 128), 1)


def upper_half():
    return lax.broadcasted_iota(jnp.int32, (8, 128), 0) < 4


def swap(value):
    return pltpu.roll(value, 4, 0)


def turn(value, shift):
    return pltpu.roll(value, shift, 1)


def primitives(state, direction):
    inverse = 1.0 / state[0]
    speeds = [state[1 + k] * inverse for k in range(3)]
    kinetic = state[1] * speeds[0] + state[2] * speeds[1] + state[3] * speeds[2]
    pressure = (GAS - 1.0) * (state[4] - 0.5 * kinetic)
    return inverse, speeds[direction], pressure


def fluxes(state, speed, pressure, direction):
    columns = [state[1 + direction]]
    for k in range(3):
        entry = state[1 + k] * speed
        columns.append(entry + pressure if k == direction else entry)
    columns.append((state[4] + pressure) * speed)
    return columns


def wave(inverse, speed, pressure):
    return jnp.abs(speed) + jnp.sqrt(GAS * pressure * inverse)


def lift(own, own_flux, own_wave, other, direction, sign):
    inverse, speed, pressure = primitives(other, direction)
    other_flux = fluxes(other, speed, pressure, direction)
    top = jnp.maximum(own_wave, wave(inverse, speed, pressure))
    return [
        3.0 * (sign * (other_flux[v] - own_flux[v]) + top * (other[v] - own[v])) for v in range(5)
    ]


def derivative(values):
    out = []
    for i in range(4):
        row = []
        for v in range(5):
            total = None
            for j in range(4):
                if abs(D[i][j]) > 1e-12:
                    term = (-D[i][j]) * values[j][v]
                    total = term if total is None else total + term
            row.append(total)
        out.append(row)
    return out


def strided(ref, at, v, pair, c):
    return ref[at, v, pl.ds(32 * pair + c, 8, 4), :]


def rows(ref, at, v, start):
    return ref[at, v, pl.ds(start, 8), :]


def pass_z(u, at, before, after, out, to, tile):
    lane = lanes()
    base = lax.rem(48 * tile, 80)
    place = lane + base
    first = (place == 0) | (place == 80) | (place == 160)
    last = (place == 79) | (place == 159)
    for pair in range(2):
        state = [[strided(u, at, v, pair, c) for v in range(5)] for c in range(4)]
        prims = [primitives(state[c], 2) for c in range(4)]
        flux = [fluxes(state[c], prims[c][1], prims[c][2], 2) for c in range(4)]
        rate = derivative(flux)
        left = []
        right = []
        for v in range(5):
            back = strided(u, before, v, pair, 3)
            ahead = strided(u, after, v, pair, 3)
            near = turn(jnp.where(lane == 127, back, state[3][v]), 1)
            far = turn(jnp.where(lane >= 79, state[3][v], ahead), 49)
            left.append(jnp.where(first, far, near))
            back = strided(u, before, v, pair, 0)
            ahead = strided(u, after, v, pair, 0)
            near = turn(jnp.where(lane == 0, ahead, state[0][v]), 127)
            far = turn(jnp.where(lane >= 49, back, state[0][v]), 79)
            right.append(jnp.where(last, far, near))
        low = lift(state[0], flux[0], wave(*prims[0]), left, 2, 1.0)
        high = lift(state[3], flux[3], wave(*prims[3]), right, 2, -1.0)
        for v in range(5):
            for c in range(4):
                value = rate[c][v]
                if c == 0:
                    value = value + low[v]
                if c == 3:
                    value = value + high[v]
                out[to, v, pl.ds(32 * pair + c, 8, 4), :] = value


def pass_y(u, at, before, after, out, to):
    lane = lanes()
    half = upper_half()
    sign = jnp.where(half, 1.0, -1.0).astype(jnp.float32)

    def two(x, y):
        return jnp.where(half, jnp.float32(-x), jnp.float32(-y))

    mix_low = [two(D[0][0], D[1][1]), two(D[0][1], D[1][0]), two(D[0][2], D[1][3]), two(D[0][3], D[1][2])]
    mix_high = [two(D[2][0], D[3][1]), two(D[2][1], D[3][0]), two(D[2][2], D[3][3]), two(D[2][3], D[3][2])]
    for a in range(4):
        low = [rows(u, at, v, 16 * a) for v in range(5)]
        high = [rows(u, at, v, 16 * a + 8) for v in range(5)]
        prim_low = primitives(low, 1)
        prim_high = primitives(high, 1)
        flux_low = fluxes(low, prim_low[1], prim_low[2], 1)
        flux_high = fluxes(high, prim_high[1], prim_high[2], 1)
        own = [jnp.where(half, low[v], high[v]) for v in range(5)]
        own_flux = [jnp.where(half, flux_low[v], flux_high[v]) for v in range(5)]
        own_wave = wave(*[jnp.where(half, x, y) for x, y in zip(prim_low, prim_high)])
        other = []
        for v in range(5):
            back = rows(u, before, v, 16 * a + 8)
            ahead = rows(u, after, v, 16 * a)
            down = turn(jnp.where(lane >= 48, back, high[v]), 80)
            up = turn(jnp.where(lane >= 80, low[v], ahead), 48)
            other.append(swap(jnp.where(half, up, down)))
        face = lift(own, own_flux, own_wave, other, 1, sign)
        for v in range(5):
            parts = [flux_low[v], swap(flux_low[v]), flux_high[v], swap(flux_high[v])]
            sum_low = jnp.where(half, face[v], 0.0)
            sum_high = jnp.where(half, 0.0, face[v])
            for k in range(4):
                sum_low = sum_low + mix_low[k] * parts[k]
                sum_high = sum_high + mix_high[k] * parts[k]
            out[to, v, pl.ds(16 * a, 8), :] += sum_low
            out[to, v, pl.ds(16 * a + 8, 8), :] += sum_high


def pass_x(u, at, out, to):
    for h in range(2):
        state = [[rows(u, at, v, 16 * a + 8 * h) for v in range(5)] for a in range(4)]
        flux = []
        for a in range(4):
            _, speed, pressure = primitives(state[a], 0)
            flux.append(fluxes(state[a], speed, pressure, 0))
        rate = derivative(flux)
        for a in range(4):
            for v in range(5):
                out[to, v, pl.ds(16 * a + 8 * h, 8), :] += rate[a][v]


def faces_x(u, at, lower, low_at, upper, up_at, out, to):
    for h in range(2):
        for a, other, sign in ((0, lower, 1.0), (3, upper, -1.0)):
            own = [rows(u, at, v, 16 * a + 8 * h) for v in range(5)]
            inverse, speed, pressure = primitives(own, 0)
            own_flux = fluxes(own, speed, pressure, 0)
            trace = [other(v, h) for v in range(5)]
            face = lift(own, own_flux, wave(inverse, speed, pressure), trace, 0, sign)
            for v in range(5):
                out[to, v, pl.ds(16 * a + 8 * h, 8), :] += face[v]


def inner_rate(u, at, before, after, out, to, tile):
    pass_z(u, at, before, after, out, to, tile)
    pass_y(u, at, before, after, out, to)
    pass_x(u, at, out, to)


def pack(ref, at, side, tile):
    lane = lanes()
    half = upper_half()
    packed = []
    for v in range(5):
        for pair in range(2):
            if side == 0:
                one = rows(ref, at, v, 32 * pair + 8)
                two = rows(ref, at, v, 32 * pair + 24)
                main = jnp.where(half, swap(one), two)
            else:
                one = rows(ref, at, v, 32 * pair)
                two = rows(ref, at, v, 32 * pair + 16)
                main = jnp.where(half, one, swap(two))
            if tile is not None:
                c0 = strided(ref, at, v, pair, 0)
                c3 = strided(ref, at, v, pair, 3)
                if side == 0:
                    main = jnp.where(lane == 0, turn(c0, 8 + 8 * tile), main)
                    main = jnp.where(lane == 1, turn(c3, 2), main)
                else:
                    main = jnp.where(lane == 127, turn(c0, 127), main)
                    main = jnp.where(lane == 126, turn(c3, 47 + 8 * tile), main)
            packed.append(main)
    return packed


def unpack(packed, ref, at, side, columns):
    for v in range(5):
        for pair in range(2):
            block = packed[2 * v + pair]
            if columns:
                at0, at3 = (0, 1) if side == 0 else (127, 126)
                c0 = jnp.broadcast_to(block[:, at0 : at0 + 1], (8, 128))
                c3 = jnp.broadcast_to(block[:, at3 : at3 + 1], (8, 128))
                ref[at, v, pl.ds(32 * pair, 8, 4), :] = c0
                ref[at, v, pl.ds(32 * pair + 3, 8, 4), :] = c3
            shift = 12 if side == 0 else 0
            ref[at, v, pl.ds(32 * pair + shift, 4), :] = block[0:4]
            ref[at, v, pl.ds(32 * pair + 16 + shift, 4), :] = block[4:8]


MID_FIRST = 1


def kernel(
    start_hbm,
    offset_hbm,
    out_hbm,
    start,
    u0,
    x_low,
    x_high,
    rate,
    halo_send,
    landed,
    halo,
    u1,
    x_low2,
    x_high2,
    rate2,
    give,
    pair_send,
    pair_land,
    load_sem,
    x_send,
    x_recv,
    mid_send,
    mid_recv,
    end_send,
    end_recv,
    halo_ssem,
    halo_rsem,
    own_sem,
    own_halo_sem,
    x_send2,
    x_recv2,
    give_send,
    give_recv,
    give_own,
    pair_ssem,
    pair_rsem,
):
    m = lax.axis_index("node")
    s = lax.axis_index("space")
    hi = (s // 8) % 2
    q = m + hi * (3 - 2 * m)
    odd = q % 2
    left = 1 - q // 2
    up = (s + 1) % 64
    down = (s + 63) % 64
    hi_up = (up // 8) % 2
    hi_down = (down // 8) % 2
    q_up = q + hi_up * (3 - 2 * q)
    q_down = q + hi_down * (3 - 2 * q)
    slot_from = (3 - q) // 3
    slot_to = 3 - q // 3
    first_tile = 3 * q - 1
    k_from = 1 - (q % 3 + 1) // 2
    other_q = q + 1 - 2 * odd
    partner = other_q + hi * (3 - 2 * other_q)

    def turn_of(i):
        g = i % 5
        near = (g % 2) * ((g - 1) // 2) + (1 - g % 2) * (4 - g // 2)
        flip = (i // 5 + left) % 2
        return near + flip * (9 - 2 * near)

    def place_of(d):
        return d + hi * (3 - 2 * d)

    def loads(t):
        return (
            pltpu.make_async_copy(start_hbm.at[:, :, t, 0, :], start.at[t], load_sem.at[0, t]),
            pltpu.make_async_copy(offset_hbm.at[:, :, t, 0, :], u0.at[t], load_sem.at[1, t]),
        )

    def begin(i, carry):
        one, two = loads(turn_of(i))
        one.start()
        two.start()
        return carry

    lax.fori_loop(0, TILES, begin, 0)

    barrier = pltpu.get_barrier_semaphore()
    for k in range(1, 4):
        pl.semaphore_signal(barrier, inc=1, device_id={"node": (m + k) % 4}, device_id_type=MESH)
    pl.semaphore_signal(barrier, inc=1, device_id={"space": up}, device_id_type=MESH)
    pl.semaphore_signal(barrier, inc=1, device_id={"space": down}, device_id_type=MESH)
    pl.semaphore_signal(barrier, inc=1, device_id={"node": q_up, "space": up}, device_id_type=MESH)
    pl.semaphore_signal(barrier, inc=1, device_id={"node": q_down, "space": down}, device_id_type=MESH)
    pl.semaphore_wait(barrier, 7)

    def x_copies(t):
        return (
            pltpu.make_async_remote_copy(
                src_ref=u0.at[t, :, pl.ds(48, 16)],
                dst_ref=x_low.at[t],
                send_sem=x_send.at[0, t],
                recv_sem=x_recv.at[0, t],
                device_id={"space": up},
                device_id_type=MESH,
            ),
            pltpu.make_async_remote_copy(
                src_ref=u0.at[t, :, pl.ds(0, 16)],
                dst_ref=x_high.at[t],
                send_sem=x_send.at[1, t],
                recv_sem=x_recv.at[1, t],
                device_id={"space": down},
                device_id_type=MESH,
            ),
        )

    def guess(i, carry):
        t = turn_of(i)
        one, two = loads(t)
        one.wait()
        two.wait()
        for v in range(5):
            u0[t, v] = u0[t, v] + start[t, v]
        one, two = x_copies(t)
        one.start()
        two.start()
        return carry

    lax.fori_loop(0, TILES, guess, 0)

    def owner(t):
        return (t + 1) // 3

    def mid_copy(t):
        d = owner(t)
        slot = t - 3 * d + 1
        return pltpu.make_async_remote_copy(
            src_ref=rate.at[t, :, pl.ds(16, 32)],
            dst_ref=landed.at[m, slot, :, pl.ds(16, 32)],
            send_sem=mid_send.at[t],
            recv_sem=mid_recv.at[m, slot],
            device_id={"node": place_of(d)},
            device_id_type=MESH,
        )

    def end_copies(t):
        d = owner(t)
        slot = t - 3 * d + 1
        return [
            pltpu.make_async_remote_copy(
                src_ref=rate.at[t, :, pl.ds(48 * k, 16)],
                dst_ref=landed.at[m, slot, :, pl.ds(48 * k, 16)],
                send_sem=end_send.at[k, t],
                recv_sem=end_recv.at[k, m, slot],
                device_id={"node": place_of(d)},
                device_id_type=MESH,
            )
            for k in range(2)
        ]

    def own_copy(slot):
        return pltpu.make_async_copy(
            rate.at[first_tile + slot], landed.at[m, slot], own_sem.at[slot]
        )

    def send_mid(i):
        t = turn_of(i)

        @pl.when(owner(t) != q)
        def _():
            mid_copy(t).start()

    def inside(i, carry):
        t = turn_of(i)
        inner_rate(u0, t, (t + 9) % 10, (t + 1) % 10, rate, t, t)

        @pl.when(i < MID_FIRST)
        def _():
            send_mid(i)

        return carry

    lax.fori_loop(0, TILES, inside, 0)

    def edges(i, carry):
        t = turn_of(i)
        one, two = x_copies(t)
        one.wait_recv()
        two.wait_recv()
        faces_x(
            u0,
            t,
            lambda v, h: x_low[t, v, pl.ds(8 * h, 8), :],
            t,
            lambda v, h: x_high[t, v, pl.ds(8 * h, 8), :],
            t,
            rate,
            t,
        )

        @pl.when(owner(t) != q)
        def _():
            for copy in end_copies(t):
                copy.start()

        @pl.when(owner(t) == q)
        def _():
            own_copy(t - first_tile).start()

        return carry

    lax.fori_loop(0, TILES, edges, 0)

    def halo_copy(d):
        return pltpu.make_async_remote_copy(
            src_ref=halo_send.at[d],
            dst_ref=halo.at[m],
            send_sem=halo_ssem.at[d],
            recv_sem=halo_rsem.at[m],
            device_id={"node": place_of(d)},
            device_id_type=MESH,
        )

    own_halo = pltpu.make_async_copy(halo_send.at[q], halo.at[m], own_halo_sem)

    for d, side, tile in ((0, 0, 9), (1, 1, 5), (2, 0, 4), (3, 1, 0)):
        for k, block in enumerate(pack(rate, tile, side, None)):
            halo_send[d, pl.ds(8 * k, 8), :] = block

    def borders(d, carry):
        @pl.when(d != q)
        def _():
            halo_copy(d).start()

        return carry

    lax.fori_loop(0, 4, borders, 0)
    own_halo.start()

    def rest(i, carry):
        send_mid(i)
        return carry

    lax.fori_loop(MID_FIRST, TILES, rest, 0)

    def arrived(part, sem):
        pltpu.make_async_remote_copy(
            src_ref=part,
            dst_ref=part,
            send_sem=mid_send.at[0],
            recv_sem=sem,
            device_id={"node": (m + 1) % 4},
            device_id_type=MESH,
        ).wait_recv()

    def x_copies2(slot):
        return (
            pltpu.make_async_remote_copy(
                src_ref=u1.at[:, slot + 1, :, pl.ds(48, 16)],
                dst_ref=x_low2.at[slot],
                send_sem=x_send2.at[0, slot],
                recv_sem=x_recv2.at[0, slot],
                device_id={"node": q_up, "space": up},
                device_id_type=MESH,
            ),
            pltpu.make_async_remote_copy(
                src_ref=u1.at[:, slot + 1, :, pl.ds(0, 16)],
                dst_ref=x_high2.at[slot],
                send_sem=x_send2.at[1, slot],
                recv_sem=x_recv2.at[1, slot],
                device_id={"node": q_down, "space": down},
                device_id_type=MESH,
            ),
        )

    def advance(slot, offset, stride):
        def each(v, inner):
            for part in range(4):
                at = offset + 8 * (part % 2) + stride * (part // 2)
                held = [landed[j, slot, v, pl.ds(at, 8), :] for j in range(4)]
                base = start[first_tile + slot, v, pl.ds(at, 8), :]
                for k in range(4):
                    total = Q[k][0] * held[0]
                    for j in range(1, 4):
                        total = total + Q[k][j] * held[j]
                    u1[k, slot + 1, v, pl.ds(at, 8), :] = base + total
            return inner

        lax.fori_loop(0, 5, each, 0)

    def next_state(slot):
        def ends(j, carry):
            @pl.when(j != m)
            def _():
                for k in range(2):
                    arrived(landed.at[j, slot, :, pl.ds(48 * k, 16)], end_recv.at[k, j, slot])

            return carry

        own_copy(slot).wait()
        lax.fori_loop(0, 4, ends, 0)
        advance(slot, 0, 48)
        one, two = x_copies2(slot)
        one.start()
        two.start()

        def mids(j, carry):
            @pl.when(j != m)
            def _():
                arrived(landed.at[j, slot, :, pl.ds(16, 32)], mid_recv.at[j, slot])

            return carry

        lax.fori_loop(0, 4, mids, 0)
        advance(slot, 16, 16)

    def middle_rows():
        def wait(j, carry):
            @pl.when(j != m)
            def _():
                arrived(halo.at[j], halo_rsem.at[j])

            return carry

        own_halo.wait()
        lax.fori_loop(0, 4, wait, 0)

        def fill(side, tile, at):
            base = pack(start, tile, side, None)
            held = [[halo[j, pl.ds(8 * k, 8), :] for k in range(10)] for j in range(4)]
            for node in range(4):
                blocks = []
                for k in range(10):
                    total = Q[node][0] * held[0][k]
                    for j in range(1, 4):
                        total = total + Q[node][j] * held[j][k]
                    blocks.append(base[k] + total)
                unpack(blocks, u1.at[node], at, side, False)

        @pl.when(odd == 0)
        def _():
            fill(0, (first_tile + slot_from + 9) % 10, slot_from)

        @pl.when(odd == 1)
        def _():
            fill(1, (first_tile + slot_to) % 10, slot_to + 1)

    pair_copy = pltpu.make_async_remote_copy(
        src_ref=pair_send,
        dst_ref=pair_land,
        send_sem=pair_ssem,
        recv_sem=pair_rsem,
        device_id={"node": partner},
        device_id_type=MESH,
    )

    def pair_out(slot):
        def give_rows(side):
            def each(node, carry):
                blocks = pack(u1.at[node], slot + 1, side, first_tile + slot)
                for k, block in enumerate(blocks):
                    pair_send[node, pl.ds(8 * k, 8), :] = block
                return carry

            lax.fori_loop(0, 4, each, 0)

        @pl.when(odd == 0)
        def _():
            give_rows(0)

        @pl.when(odd == 1)
        def _():
            give_rows(1)

        pair_copy.start()

    def pair_in():
        pair_copy.wait_recv()

        def take_rows(side, at):
            def each(node, carry):
                blocks = [pair_land[node, pl.ds(8 * k, 8), :] for k in range(10)]
                unpack(blocks, u1.at[node], at, side, True)
                return carry

            lax.fori_loop(0, 4, each, 0)

        @pl.when(odd == 0)
        def _():
            take_rows(1, slot_to + 1)

        @pl.when(odd == 1)
        def _():
            take_rows(0, slot_from)

    def give_copy(node, slot):
        return pltpu.make_async_remote_copy(
            src_ref=give.at[node, slot],
            dst_ref=out_hbm.at[:, :, first_tile + slot, 0, :],
            send_sem=give_send.at[node, slot],
            recv_sem=give_recv.at[first_tile + slot],
            device_id={"node": node},
            device_id_type=MESH,
        )

    def give_here(slot):
        return pltpu.make_async_copy(
            give.at[m, slot], out_hbm.at[:, :, first_tile + slot, 0, :], give_own.at[slot]
        )

    def second(slot):
        def each(node, carry):
            inner_rate(
                u1.at[node], slot + 1, slot, slot + 2, rate2.at[node], slot, first_tile + slot
            )
            return carry

        lax.fori_loop(0, 4, each, 0)
        one, two = x_copies2(slot)
        one.wait_recv()
        two.wait_recv()

        def edge(node, carry):
            faces_x(
                u1.at[node],
                slot + 1,
                lambda v, h: x_low2[slot, node, v, pl.ds(8 * h, 8), :],
                slot,
                lambda v, h: x_high2[slot, node, v, pl.ds(8 * h, 8), :],
                slot,
                rate2.at[node],
                slot,
            )
            return carry

        lax.fori_loop(0, 4, edge, 0)

        def gather(v, carry):
            for part in range(8):
                held = [rate2[j, slot, v, pl.ds(8 * part, 8), :] for j in range(4)]
                for k in range(4):
                    total = Q[k][0] * held[0]
                    for j in range(1, 4):
                        total = total + Q[k][j] * held[j]
                    give[k, slot, v, pl.ds(8 * part, 8), :] = total
            return carry

        lax.fori_loop(0, 5, gather, 0)

        def send(k, carry):
            node = (m + 2 + k) % 4

            @pl.when(node != m)
            def _():
                give_copy(node, slot).start()

            @pl.when(node == m)
            def _():
                give_here(slot).start()

            return carry

        lax.fori_loop(0, 4, send, 0)

    def slot_of(k):
        return k + odd * (2 - 2 * k)

    def stage(k, carry):
        @pl.when(k < 3)
        def _():
            next_state(slot_of(k))

        @pl.when(k == k_from)
        def _():
            middle_rows()

        @pl.when(k == 2)
        def _():
            pair_out(slot_of(k))

        @pl.when(k == 3)
        def _():
            pair_in()

        @pl.when(k > k_from)
        def _():
            second(slot_of(k - 1))

        return carry

    lax.fori_loop(k_from, 4, stage, 0)

    def drain(t, carry):
        one, two = x_copies(t)
        one.wait_send()
        two.wait_send()

        @pl.when(owner(t) != q)
        def _():
            mid_copy(t).wait_send()
            for copy in end_copies(t):
                copy.wait_send()
            arrived(out_hbm.at[:, :, t, 0, :], give_recv.at[t])

        return carry

    lax.fori_loop(0, TILES, drain, 0)

    def drain_nodes(d, carry):
        @pl.when(d != q)
        def _():
            halo_copy(d).wait_send()

        return carry

    lax.fori_loop(0, 4, drain_nodes, 0)
    pair_copy.wait_send()

    def drain_slots(slot, carry):
        one, two = x_copies2(slot)
        one.wait_send()
        two.wait_send()
        give_here(slot).wait()

        def each(node, inner):
            @pl.when(node != m)
            def _():
                give_copy(node, slot).wait_send()

            return inner

        lax.fori_loop(0, 4, each, 0)
        return carry

    lax.fori_loop(slot_from, slot_to, drain_slots, 0)


def body(start_state, node_offset):
    flat = (5, 64, TILES, 1, 128)
    vmem = lambda *shape: pltpu.VMEM(shape, jnp.float32)
    dma = lambda *shape: pltpu.SemaphoreType.DMA(shape)
    out = pl.pallas_call(
        kernel,
        out_shape=jax.ShapeDtypeStruct(flat, jnp.float32),
        in_specs=[pl.BlockSpec(memory_space=pltpu.HBM)] * 2,
        out_specs=pl.BlockSpec(memory_space=pl.ANY),
        scratch_shapes=[
            vmem(10, 5, 64, 128),
            vmem(10, 5, 64, 128),
            vmem(10, 5, 16, 128),
            vmem(10, 5, 16, 128),
            vmem(10, 5, 64, 128),
            vmem(4, 80, 128),
            vmem(4, 3, 5, 64, 128),
            vmem(4, 80, 128),
            vmem(4, 5, 5, 64, 128),
            vmem(3, 4, 5, 16, 128),
            vmem(3, 4, 5, 16, 128),
            vmem(4, 3, 5, 64, 128),
            vmem(4, 3, 5, 64, 128),
            vmem(4, 80, 128),
            vmem(4, 80, 128),
            dma(2, 10),
            dma(2, 10),
            dma(2, 10),
            dma(10),
            dma(4, 3),
            dma(2, 10),
            dma(2, 4, 3),
            dma(4),
            dma(4),
            dma(3),
            pltpu.SemaphoreType.DMA,
            dma(2, 3),
            dma(2, 3),
            dma(4, 3),
            dma(10),
            dma(3),
            pltpu.SemaphoreType.DMA,
            pltpu.SemaphoreType.DMA,
        ],
        compiler_params=pltpu.CompilerParams(
            collective_id=0, has_side_effects=True, vmem_limit_bytes=52 << 20
        ),
    )(start_state.reshape(flat), node_offset.reshape(flat))
    return out.reshape((1,) + start_state.shape)


def solution(mesh):
    return jax.shard_map(
        body,
        mesh=mesh,
        in_specs=(
            P(None, None, None, None, "space", None),
            P("node", None, None, None, None, "space", None),
        ),
        out_specs=P("node", None, None, None, None, "space", None),
        check_vma=False,
    )
```

```python
import functools
import math

import jax
import jax.numpy as jnp
import numpy as np
from jax import lax
from jax.experimental import pallas as pl
from jax.experimental.pallas import tpu as pltpu
from jax.sharding import PartitionSpec as P

MESH = pl.DeviceIdType.MESH
TILES = 10
GAS = 1.4
STEP = 0.01


def lobatto_derivative():
    points = np.array([-1.0, -math.sqrt(0.2), math.sqrt(0.2), 1.0])
    barycentric = np.ones(4)
    for i in range(4):
        for k in range(4):
            if k != i:
                barycentric[i] = barycentric[i] / (points[i] - points[k])
    derivative = np.zeros((4, 4))
    for i in range(4):
        for j in range(4):
            if i != j:
                derivative[i, j] = barycentric[j] / barycentric[i] / (points[i] - points[j])
        derivative[i, i] = -np.sum(derivative[i])
    return derivative


def collocation_matrix():
    near_root = math.sqrt(3.0 / 7 - 2.0 / 7 * math.sqrt(1.2))
    far_root = math.sqrt(3.0 / 7 + 2.0 / 7 * math.sqrt(1.2))
    time_nodes = [(1.0 + value) / 2 for value in (-far_root, -near_root, near_root, far_root)]
    quad_table = np.zeros((4, 4))
    for j in range(4):
        coeffs = [1.0]
        for k in range(4):
            if k != j:
                scale = 1.0 / (time_nodes[j] - time_nodes[k])
                widened = [0.0] * (len(coeffs) + 1)
                for power in range(len(coeffs)):
                    widened[power + 1] = widened[power + 1] + coeffs[power] * scale
                    widened[power] = widened[power] - time_nodes[k] * coeffs[power] * scale
                coeffs = widened
        for m in range(4):
            total = 0.0
            for power in range(len(coeffs)):
                total = total + coeffs[power] * time_nodes[m] ** (power + 1) / (power + 1)
            quad_table[m, j] = total
    return quad_table


D = [[float(value) for value in row] for row in lobatto_derivative()]
Q = [[float(STEP * value) for value in row] for row in collocation_matrix()]


def lanes():
    return lax.broadcasted_iota(jnp.int32, (8, 128), 1)


def upper_half():
    return lax.broadcasted_iota(jnp.int32, (8, 128), 0) < 4


def swap(value):
    return pltpu.roll(value, 4, 0)


def turn(value, shift):
    return pltpu.roll(value, shift, 1)


def primitives(state, direction):
    inverse = 1.0 / state[0]
    speeds = [state[1 + k] * inverse for k in range(3)]
    kinetic = state[1] * speeds[0] + state[2] * speeds[1] + state[3] * speeds[2]
    pressure = (GAS - 1.0) * (state[4] - 0.5 * kinetic)
    return inverse, speeds[direction], pressure


def fluxes(state, speed, pressure, direction):
    columns = [state[1 + direction]]
    for k in range(3):
        entry = state[1 + k] * speed
        columns.append(entry + pressure if k == direction else entry)
    columns.append((state[4] + pressure) * speed)
    return columns


def wave(inverse, speed, pressure):
    return jnp.abs(speed) + jnp.sqrt(GAS * pressure * inverse)


def lift(own, own_flux, own_wave, other, direction, sign):
    inverse, speed, pressure = primitives(other, direction)
    other_flux = fluxes(other, speed, pressure, direction)
    top = jnp.maximum(own_wave, wave(inverse, speed, pressure))
    return [
        3.0 * (sign * (other_flux[v] - own_flux[v]) + top * (other[v] - own[v])) for v in range(5)
    ]


def derivative(values):
    out = []
    for i in range(4):
        row = []
        for v in range(5):
            total = None
            for j in range(4):
                if abs(D[i][j]) > 1e-12:
                    term = (-D[i][j]) * values[j][v]
                    total = term if total is None else total + term
            row.append(total)
        out.append(row)
    return out


def strided(ref, at, v, pair, c):
    return ref[at, v, pl.ds(32 * pair + c, 8, 4), :]


def rows(ref, at, v, start):
    return ref[at, v, pl.ds(start, 8), :]


def pass_z(u, at, before, after, out, to, tile):
    lane = lanes()
    base = lax.rem(48 * tile, 80)
    place = lane + base
    first = (place == 0) | (place == 80) | (place == 160)
    last = (place == 79) | (place == 159)
    for pair in range(2):
        state = [[strided(u, at, v, pair, c) for v in range(5)] for c in range(4)]
        prims = [primitives(state[c], 2) for c in range(4)]
        flux = [fluxes(state[c], prims[c][1], prims[c][2], 2) for c in range(4)]
        rate = derivative(flux)
        left = []
        right = []
        for v in range(5):
            back = strided(u, before, v, pair, 3)
            ahead = strided(u, after, v, pair, 3)
            near = turn(jnp.where(lane == 127, back, state[3][v]), 1)
            far = turn(jnp.where(lane >= 79, state[3][v], ahead), 49)
            left.append(jnp.where(first, far, near))
            back = strided(u, before, v, pair, 0)
            ahead = strided(u, after, v, pair, 0)
            near = turn(jnp.where(lane == 0, ahead, state[0][v]), 127)
            far = turn(jnp.where(lane >= 49, back, state[0][v]), 79)
            right.append(jnp.where(last, far, near))
        low = lift(state[0], flux[0], wave(*prims[0]), left, 2, 1.0)
        high = lift(state[3], flux[3], wave(*prims[3]), right, 2, -1.0)
        for v in range(5):
            for c in range(4):
                value = rate[c][v]
                if c == 0:
                    value = value + low[v]
                if c == 3:
                    value = value + high[v]
                out[to, v, pl.ds(32 * pair + c, 8, 4), :] = value


def pass_y(u, at, before, after, out, to):
    lane = lanes()
    half = upper_half()
    sign = jnp.where(half, 1.0, -1.0).astype(jnp.float32)

    def two(x, y):
        return jnp.where(half, jnp.float32(-x), jnp.float32(-y))

    mix_low = [two(D[0][0], D[1][1]), two(D[0][1], D[1][0]), two(D[0][2], D[1][3]), two(D[0][3], D[1][2])]
    mix_high = [two(D[2][0], D[3][1]), two(D[2][1], D[3][0]), two(D[2][2], D[3][3]), two(D[2][3], D[3][2])]
    for a in range(4):
        low = [rows(u, at, v, 16 * a) for v in range(5)]
        high = [rows(u, at, v, 16 * a + 8) for v in range(5)]
        prim_low = primitives(low, 1)
        prim_high = primitives(high, 1)
        flux_low = fluxes(low, prim_low[1], prim_low[2], 1)
        flux_high = fluxes(high, prim_high[1], prim_high[2], 1)
        own = [jnp.where(half, low[v], high[v]) for v in range(5)]
        own_flux = [jnp.where(half, flux_low[v], flux_high[v]) for v in range(5)]
        own_wave = wave(*[jnp.where(half, x, y) for x, y in zip(prim_low, prim_high)])
        other = []
        for v in range(5):
            back = rows(u, before, v, 16 * a + 8)
            ahead = rows(u, after, v, 16 * a)
            down = turn(jnp.where(lane >= 48, back, high[v]), 80)
            up = turn(jnp.where(lane >= 80, low[v], ahead), 48)
            other.append(swap(jnp.where(half, up, down)))
        face = lift(own, own_flux, own_wave, other, 1, sign)
        for v in range(5):
            parts = [flux_low[v], swap(flux_low[v]), flux_high[v], swap(flux_high[v])]
            sum_low = jnp.where(half, face[v], 0.0)
            sum_high = jnp.where(half, 0.0, face[v])
            for k in range(4):
                sum_low = sum_low + mix_low[k] * parts[k]
                sum_high = sum_high + mix_high[k] * parts[k]
            out[to, v, pl.ds(16 * a, 8), :] += sum_low
            out[to, v, pl.ds(16 * a + 8, 8), :] += sum_high


def pass_x(u, at, out, to):
    for h in range(2):
        state = [[rows(u, at, v, 16 * a + 8 * h) for v in range(5)] for a in range(4)]
        flux = []
        for a in range(4):
            _, speed, pressure = primitives(state[a], 0)
            flux.append(fluxes(state[a], speed, pressure, 0))
        rate = derivative(flux)
        for a in range(4):
            for v in range(5):
                out[to, v, pl.ds(16 * a + 8 * h, 8), :] += rate[a][v]


def faces_x(u, at, lower, low_at, upper, up_at, out, to):
    for h in range(2):
        for a, other, sign in ((0, lower, 1.0), (3, upper, -1.0)):
            own = [rows(u, at, v, 16 * a + 8 * h) for v in range(5)]
            inverse, speed, pressure = primitives(own, 0)
            own_flux = fluxes(own, speed, pressure, 0)
            trace = [other(v, h) for v in range(5)]
            face = lift(own, own_flux, wave(inverse, speed, pressure), trace, 0, sign)
            for v in range(5):
                out[to, v, pl.ds(16 * a + 8 * h, 8), :] += face[v]


def inner_rate(u, at, before, after, out, to, tile):
    pass_z(u, at, before, after, out, to, tile)
    pass_y(u, at, before, after, out, to)
    pass_x(u, at, out, to)


def pack(ref, at, side, tile):
    lane = lanes()
    half = upper_half()
    packed = []
    for v in range(5):
        for pair in range(2):
            if side == 0:
                one = rows(ref, at, v, 32 * pair + 8)
                two = rows(ref, at, v, 32 * pair + 24)
                main = jnp.where(half, swap(one), two)
            else:
                one = rows(ref, at, v, 32 * pair)
                two = rows(ref, at, v, 32 * pair + 16)
                main = jnp.where(half, one, swap(two))
            if tile is not None:
                c0 = strided(ref, at, v, pair, 0)
                c3 = strided(ref, at, v, pair, 3)
                if side == 0:
                    main = jnp.where(lane == 0, turn(c0, 8 + 8 * tile), main)
                    main = jnp.where(lane == 1, turn(c3, 2), main)
                else:
                    main = jnp.where(lane == 127, turn(c0, 127), main)
                    main = jnp.where(lane == 126, turn(c3, 47 + 8 * tile), main)
            packed.append(main)
    return packed


def unpack(packed, ref, at, side, columns):
    for v in range(5):
        for pair in range(2):
            block = packed[2 * v + pair]
            if columns:
                at0, at3 = (0, 1) if side == 0 else (127, 126)
                c0 = jnp.broadcast_to(block[:, at0 : at0 + 1], (8, 128))
                c3 = jnp.broadcast_to(block[:, at3 : at3 + 1], (8, 128))
                ref[at, v, pl.ds(32 * pair, 8, 4), :] = c0
                ref[at, v, pl.ds(32 * pair + 3, 8, 4), :] = c3
            shift = 12 if side == 0 else 0
            ref[at, v, pl.ds(32 * pair + shift, 4), :] = block[0:4]
            ref[at, v, pl.ds(32 * pair + 16 + shift, 4), :] = block[4:8]


MID_FIRST = 3
HELPER = -2
ONWARD = 1 - HELPER


def relayed(t):
    return (t == 1) | (t == 2) | (t == 3) | (t == 7) | (t == 8) | (t == 6)


def kernel(
    start_hbm,
    offset_hbm,
    out_hbm,
    start,
    u0,
    x_low,
    x_high,
    rate,
    halo_send,
    landed,
    halo,
    u1,
    x_low2,
    x_high2,
    rate2,
    give,
    pair_send,
    pair_land,
    relay,
    load_sem,
    x_send,
    x_recv,
    mid_send,
    mid_recv,
    end_send,
    end_recv,
    halo_ssem,
    halo_rsem,
    own_sem,
    own_halo_sem,
    x_send2,
    x_recv2,
    give_send,
    give_recv,
    give_own,
    pair_ssem,
    pair_rsem,
    relay_send,
    relay_recv,
    onward_send,
):
    m = lax.axis_index("node")
    s = lax.axis_index("space")
    hi = (s // 8) % 2
    q = m + hi * (3 - 2 * m)
    odd = q % 2
    left = 1 - q // 2
    up = (s + 1) % 64
    down = (s + 63) % 64
    hi_up = (up // 8) % 2
    hi_down = (down // 8) % 2
    q_up = q + hi_up * (3 - 2 * q)
    q_down = q + hi_down * (3 - 2 * q)
    slot_from = (3 - q) // 3
    slot_to = 3 - q // 3
    first_tile = 3 * q - 1
    k_from = 1 - (q % 3 + 1) // 2
    other_q = q + 1 - 2 * odd
    partner = other_q + hi * (3 - 2 * other_q)
    far_up = s % 8 == 7
    far_down = s % 8 == 0
    helps_up = s % 8 == (7 + HELPER) % 8
    helps_down = s % 8 == (-HELPER) % 8

    def space(distance):
        return (s + 64 + distance) % 64

    def turn_of(i):
        g = i % 5
        near = (g % 2) * ((g - 1) // 2) + (1 - g % 2) * (4 - g // 2)
        flip = (i // 5 + left) % 2
        return near + flip * (9 - 2 * near)

    def place_of(d):
        return d + hi * (3 - 2 * d)

    def loads(t):
        return (
            pltpu.make_async_copy(start_hbm.at[:, :, t, 0, :], start.at[t], load_sem.at[0, t]),
            pltpu.make_async_copy(offset_hbm.at[:, :, t, 0, :], u0.at[t], load_sem.at[1, t]),
        )

    def begin(i, carry):
        one, two = loads(turn_of(i))
        one.start()
        two.start()
        return carry

    lax.fori_loop(0, TILES, begin, 0)

    barrier = pltpu.get_barrier_semaphore()
    for k in range(1, 4):
        pl.semaphore_signal(barrier, inc=1, device_id={"node": (m + k) % 4}, device_id_type=MESH)
    pl.semaphore_signal(barrier, inc=1, device_id={"space": up}, device_id_type=MESH)
    pl.semaphore_signal(barrier, inc=1, device_id={"space": down}, device_id_type=MESH)
    pl.semaphore_signal(barrier, inc=1, device_id={"node": q_up, "space": up}, device_id_type=MESH)
    pl.semaphore_signal(barrier, inc=1, device_id={"node": q_down, "space": down}, device_id_type=MESH)
    for role, friends in (
        (far_up, (HELPER, 1 - HELPER)),
        (far_down, (-HELPER, HELPER - 1)),
        (helps_up, (-HELPER, ONWARD)),
        (helps_down, (HELPER, -ONWARD)),
    ):

        @pl.when(role)
        def _(friends=friends):
            for friend in friends:
                pl.semaphore_signal(
                    barrier, inc=1, device_id={"space": space(friend)}, device_id_type=MESH
                )

    in_relay = far_up | far_down | helps_up | helps_down

    @pl.when(in_relay)
    def _():
        pl.semaphore_wait(barrier, 9)

    @pl.when(jnp.logical_not(in_relay))
    def _():
        pl.semaphore_wait(barrier, 7)


    def x_copies(t):
        return (
            pltpu.make_async_remote_copy(
                src_ref=u0.at[t, :, pl.ds(48, 16)],
                dst_ref=x_low.at[t],
                send_sem=x_send.at[0, t],
                recv_sem=x_recv.at[0, t],
                device_id={"space": up},
                device_id_type=MESH,
            ),
            pltpu.make_async_remote_copy(
                src_ref=u0.at[t, :, pl.ds(0, 16)],
                dst_ref=x_high.at[t],
                send_sem=x_send.at[1, t],
                recv_sem=x_recv.at[1, t],
                device_id={"space": down},
                device_id_type=MESH,
            ),
        )

    def relay_copies(t):
        return (
            pltpu.make_async_remote_copy(
                src_ref=u0.at[t, :, pl.ds(48, 16)],
                dst_ref=relay.at[t],
                send_sem=relay_send.at[t],
                recv_sem=relay_recv.at[t],
                device_id={"space": space(HELPER)},
                device_id_type=MESH,
            ),
            pltpu.make_async_remote_copy(
                src_ref=u0.at[t, :, pl.ds(0, 16)],
                dst_ref=relay.at[t],
                send_sem=relay_send.at[t],
                recv_sem=relay_recv.at[t],
                device_id={"space": space(-HELPER)},
                device_id_type=MESH,
            ),
        )

    def onward_copies(t):
        return (
            pltpu.make_async_remote_copy(
                src_ref=relay.at[t],
                dst_ref=x_low.at[t],
                send_sem=onward_send.at[t],
                recv_sem=x_recv.at[0, t],
                device_id={"space": space(ONWARD)},
                device_id_type=MESH,
            ),
            pltpu.make_async_remote_copy(
                src_ref=relay.at[t],
                dst_ref=x_high.at[t],
                send_sem=onward_send.at[t],
                recv_sem=x_recv.at[1, t],
                device_id={"space": space(-ONWARD)},
                device_id_type=MESH,
            ),
        )

    def guess(i, carry):
        t = turn_of(i)
        one, two = loads(t)
        one.wait()
        two.wait()
        for v in range(5):
            u0[t, v] = u0[t, v] + start[t, v]
        one, two = x_copies(t)
        by_up, by_down = relay_copies(t)

        @pl.when(far_up & relayed(t))
        def _():
            by_up.start()

        @pl.when(jnp.logical_not(far_up & relayed(t)))
        def _():
            one.start()

        @pl.when(far_down & relayed(t))
        def _():
            by_down.start()

        @pl.when(jnp.logical_not(far_down & relayed(t)))
        def _():
            two.start()

        return carry

    lax.fori_loop(0, TILES, guess, 0)

    def owner(t):
        return (t + 1) // 3

    def mid_copy(t):
        d = owner(t)
        slot = t - 3 * d + 1
        return pltpu.make_async_remote_copy(
            src_ref=rate.at[t, :, pl.ds(16, 32)],
            dst_ref=landed.at[m, slot, :, pl.ds(16, 32)],
            send_sem=mid_send.at[t],
            recv_sem=mid_recv.at[m, slot],
            device_id={"node": place_of(d)},
            device_id_type=MESH,
        )

    def end_copies(t):
        d = owner(t)
        slot = t - 3 * d + 1
        return [
            pltpu.make_async_remote_copy(
                src_ref=rate.at[t, :, pl.ds(48 * k, 16)],
                dst_ref=landed.at[m, slot, :, pl.ds(48 * k, 16)],
                send_sem=end_send.at[k, t],
                recv_sem=end_recv.at[k, m, slot],
                device_id={"node": place_of(d)},
                device_id_type=MESH,
            )
            for k in range(2)
        ]

    def own_copy(slot):
        return pltpu.make_async_copy(
            rate.at[first_tile + slot], landed.at[m, slot], own_sem.at[slot]
        )

    def send_mid(i):
        t = turn_of(i)

        @pl.when(owner(t) != q)
        def _():
            mid_copy(t).start()

    def inside(i, carry):
        t = turn_of(i)
        inner_rate(u0, t, (t + 9) % 10, (t + 1) % 10, rate, t, t)

        @pl.when(i < MID_FIRST)
        def _():
            send_mid(i)

        return carry

    lax.fori_loop(0, TILES, inside, 0)

    def onward(t, carry):
        one, two = onward_copies(t)

        @pl.when(helps_up & relayed(t))
        def _():
            relay_copies(t)[0].wait_recv()
            one.start()

        @pl.when(helps_down & relayed(t))
        def _():
            relay_copies(t)[1].wait_recv()
            two.start()

        return carry

    lax.fori_loop(1, 9, onward, 0)

    def edges(i, carry):
        t = turn_of(i)
        one, two = x_copies(t)
        one.wait_recv()
        two.wait_recv()
        faces_x(
            u0,
            t,
            lambda v, h: x_low[t, v, pl.ds(8 * h, 8), :],
            t,
            lambda v, h: x_high[t, v, pl.ds(8 * h, 8), :],
            t,
            rate,
            t,
        )

        @pl.when(owner(t) != q)
        def _():
            for copy in end_copies(t):
                copy.start()

        @pl.when(owner(t) == q)
        def _():
            own_copy(t - first_tile).start()

        return carry

    lax.fori_loop(0, TILES, edges, 0)

    def halo_copy(d):
        return pltpu.make_async_remote_copy(
            src_ref=halo_send.at[d],
            dst_ref=halo.at[m],
            send_sem=halo_ssem.at[d],
            recv_sem=halo_rsem.at[m],
            device_id={"node": place_of(d)},
            device_id_type=MESH,
        )

    own_halo = pltpu.make_async_copy(halo_send.at[q], halo.at[m], own_halo_sem)

    for d, side, tile in ((0, 0, 9), (1, 1, 5), (2, 0, 4), (3, 1, 0)):
        for k, block in enumerate(pack(rate, tile, side, None)):
            halo_send[d, pl.ds(8 * k, 8), :] = block

    def borders(d, carry):
        @pl.when(d != q)
        def _():
            halo_copy(d).start()

        return carry

    lax.fori_loop(0, 4, borders, 0)
    own_halo.start()

    def rest(i, carry):
        send_mid(i)
        return carry

    lax.fori_loop(MID_FIRST, TILES, rest, 0)

    def arrived(part, sem):
        pltpu.make_async_remote_copy(
            src_ref=part,
            dst_ref=part,
            send_sem=mid_send.at[0],
            recv_sem=sem,
            device_id={"node": (m + 1) % 4},
            device_id_type=MESH,
        ).wait_recv()

    def x_copies2(slot):
        return (
            pltpu.make_async_remote_copy(
                src_ref=u1.at[:, slot + 1, :, pl.ds(48, 16)],
                dst_ref=x_low2.at[slot],
                send_sem=x_send2.at[0, slot],
                recv_sem=x_recv2.at[0, slot],
                device_id={"node": q_up, "space": up},
                device_id_type=MESH,
            ),
            pltpu.make_async_remote_copy(
                src_ref=u1.at[:, slot + 1, :, pl.ds(0, 16)],
                dst_ref=x_high2.at[slot],
                send_sem=x_send2.at[1, slot],
                recv_sem=x_recv2.at[1, slot],
                device_id={"node": q_down, "space": down},
                device_id_type=MESH,
            ),
        )

    def advance(slot, offset, stride):
        def each(v, inner):
            for part in range(4):
                at = offset + 8 * (part % 2) + stride * (part // 2)
                held = [landed[j, slot, v, pl.ds(at, 8), :] for j in range(4)]
                base = start[first_tile + slot, v, pl.ds(at, 8), :]
                for k in range(4):
                    total = Q[k][0] * held[0]
                    for j in range(1, 4):
                        total = total + Q[k][j] * held[j]
                    u1[k, slot + 1, v, pl.ds(at, 8), :] = base + total
            return inner

        lax.fori_loop(0, 5, each, 0)

    def next_state(slot):
        def ends(j, carry):
            @pl.when(j != m)
            def _():
                for k in range(2):
                    arrived(landed.at[j, slot, :, pl.ds(48 * k, 16)], end_recv.at[k, j, slot])

            return carry

        own_copy(slot).wait()
        lax.fori_loop(0, 4, ends, 0)
        advance(slot, 0, 48)
        one, two = x_copies2(slot)
        one.start()
        two.start()

        def mids(j, carry):
            @pl.when(j != m)
            def _():
                arrived(landed.at[j, slot, :, pl.ds(16, 32)], mid_recv.at[j, slot])

            return carry

        lax.fori_loop(0, 4, mids, 0)
        advance(slot, 16, 16)

    def middle_rows():
        def wait(j, carry):
            @pl.when(j != m)
            def _():
                arrived(halo.at[j], halo_rsem.at[j])

            return carry

        own_halo.wait()
        lax.fori_loop(0, 4, wait, 0)

        def fill(side, tile, at):
            base = pack(start, tile, side, None)
            held = [[halo[j, pl.ds(8 * k, 8), :] for k in range(10)] for j in range(4)]
            for node in range(4):
                blocks = []
                for k in range(10):
                    total = Q[node][0] * held[0][k]
                    for j in range(1, 4):
                        total = total + Q[node][j] * held[j][k]
                    blocks.append(base[k] + total)
                unpack(blocks, u1.at[node], at, side, False)

        @pl.when(odd == 0)
        def _():
            fill(0, (first_tile + slot_from + 9) % 10, slot_from)

        @pl.when(odd == 1)
        def _():
            fill(1, (first_tile + slot_to) % 10, slot_to + 1)

    pair_copy = pltpu.make_async_remote_copy(
        src_ref=pair_send,
        dst_ref=pair_land,
        send_sem=pair_ssem,
        recv_sem=pair_rsem,
        device_id={"node": partner},
        device_id_type=MESH,
    )

    def pair_out(slot):
        def give_rows(side):
            def each(node, carry):
                blocks = pack(u1.at[node], slot + 1, side, first_tile + slot)
                for k, block in enumerate(blocks):
                    pair_send[node, pl.ds(8 * k, 8), :] = block
                return carry

            lax.fori_loop(0, 4, each, 0)

        @pl.when(odd == 0)
        def _():
            give_rows(0)

        @pl.when(odd == 1)
        def _():
            give_rows(1)

        pair_copy.start()

    def pair_in():
        pair_copy.wait_recv()

        def take_rows(side, at):
            def each(node, carry):
                blocks = [pair_land[node, pl.ds(8 * k, 8), :] for k in range(10)]
                unpack(blocks, u1.at[node], at, side, True)
                return carry

            lax.fori_loop(0, 4, each, 0)

        @pl.when(odd == 0)
        def _():
            take_rows(1, slot_to + 1)

        @pl.when(odd == 1)
        def _():
            take_rows(0, slot_from)

    def give_copy(node, slot):
        return pltpu.make_async_remote_copy(
            src_ref=give.at[node, slot],
            dst_ref=out_hbm.at[:, :, first_tile + slot, 0, :],
            send_sem=give_send.at[node, slot],
            recv_sem=give_recv.at[first_tile + slot],
            device_id={"node": node},
            device_id_type=MESH,
        )

    def give_here(slot):
        return pltpu.make_async_copy(
            give.at[m, slot], out_hbm.at[:, :, first_tile + slot, 0, :], give_own.at[slot]
        )

    def second(slot):
        def each(node, carry):
            inner_rate(
                u1.at[node], slot + 1, slot, slot + 2, rate2.at[node], slot, first_tile + slot
            )
            return carry

        lax.fori_loop(0, 4, each, 0)
        one, two = x_copies2(slot)
        one.wait_recv()
        two.wait_recv()

        def edge(node, carry):
            faces_x(
                u1.at[node],
                slot + 1,
                lambda v, h: x_low2[slot, node, v, pl.ds(8 * h, 8), :],
                slot,
                lambda v, h: x_high2[slot, node, v, pl.ds(8 * h, 8), :],
                slot,
                rate2.at[node],
                slot,
            )
            return carry

        lax.fori_loop(0, 4, edge, 0)

        def gather(v, carry):
            for part in range(8):
                held = [rate2[j, slot, v, pl.ds(8 * part, 8), :] for j in range(4)]
                for k in range(4):
                    total = Q[k][0] * held[0]
                    for j in range(1, 4):
                        total = total + Q[k][j] * held[j]
                    give[k, slot, v, pl.ds(8 * part, 8), :] = total
            return carry

        lax.fori_loop(0, 5, gather, 0)

        def send(k, carry):
            node = (m + 2 + k) % 4

            @pl.when(node != m)
            def _():
                give_copy(node, slot).start()

            @pl.when(node == m)
            def _():
                give_here(slot).start()

            return carry

        lax.fori_loop(0, 4, send, 0)

    def slot_of(k):
        return k + odd * (2 - 2 * k)

    def stage(k, carry):
        @pl.when(k < 3)
        def _():
            next_state(slot_of(k))

        @pl.when(k == k_from)
        def _():
            middle_rows()

        @pl.when(k == 2)
        def _():
            pair_out(slot_of(k))

        @pl.when(k == 3)
        def _():
            pair_in()

        @pl.when(k > k_from)
        def _():
            second(slot_of(k - 1))

        return carry

    lax.fori_loop(k_from, 4, stage, 0)

    def drain(t, carry):
        one, two = x_copies(t)
        by_up, by_down = relay_copies(t)
        on_up, on_down = onward_copies(t)

        @pl.when(far_up & relayed(t))
        def _():
            by_up.wait_send()

        @pl.when(jnp.logical_not(far_up & relayed(t)))
        def _():
            one.wait_send()

        @pl.when(far_down & relayed(t))
        def _():
            by_down.wait_send()

        @pl.when(jnp.logical_not(far_down & relayed(t)))
        def _():
            two.wait_send()

        @pl.when(helps_up & relayed(t))
        def _():
            on_up.wait_send()

        @pl.when(helps_down & relayed(t))
        def _():
            on_down.wait_send()

        @pl.when(owner(t) != q)
        def _():
            mid_copy(t).wait_send()
            for copy in end_copies(t):
                copy.wait_send()
            arrived(out_hbm.at[:, :, t, 0, :], give_recv.at[t])

        return carry

    lax.fori_loop(0, TILES, drain, 0)

    def drain_nodes(d, carry):
        @pl.when(d != q)
        def _():
            halo_copy(d).wait_send()

        return carry

    lax.fori_loop(0, 4, drain_nodes, 0)
    pair_copy.wait_send()

    def drain_slots(slot, carry):
        one, two = x_copies2(slot)
        one.wait_send()
        two.wait_send()
        give_here(slot).wait()

        def each(node, inner):
            @pl.when(node != m)
            def _():
                give_copy(node, slot).wait_send()

            return inner

        lax.fori_loop(0, 4, each, 0)
        return carry

    lax.fori_loop(slot_from, slot_to, drain_slots, 0)


def body(start_state, node_offset):
    flat = (5, 64, TILES, 1, 128)
    vmem = lambda *shape: pltpu.VMEM(shape, jnp.float32)
    dma = lambda *shape: pltpu.SemaphoreType.DMA(shape)
    out = pl.pallas_call(
        kernel,
        out_shape=jax.ShapeDtypeStruct(flat, jnp.float32),
        in_specs=[pl.BlockSpec(memory_space=pltpu.HBM)] * 2,
        out_specs=pl.BlockSpec(memory_space=pl.ANY),
        scratch_shapes=[
            vmem(10, 5, 64, 128),
            vmem(10, 5, 64, 128),
            vmem(10, 5, 16, 128),
            vmem(10, 5, 16, 128),
            vmem(10, 5, 64, 128),
            vmem(4, 80, 128),
            vmem(4, 3, 5, 64, 128),
            vmem(4, 80, 128),
            vmem(4, 5, 5, 64, 128),
            vmem(3, 4, 5, 16, 128),
            vmem(3, 4, 5, 16, 128),
            vmem(4, 3, 5, 64, 128),
            vmem(4, 3, 5, 64, 128),
            vmem(4, 80, 128),
            vmem(4, 80, 128),
            vmem(10, 5, 16, 128),
            dma(2, 10),
            dma(2, 10),
            dma(2, 10),
            dma(10),
            dma(4, 3),
            dma(2, 10),
            dma(2, 4, 3),
            dma(4),
            dma(4),
            dma(3),
            pltpu.SemaphoreType.DMA,
            dma(2, 3),
            dma(2, 3),
            dma(4, 3),
            dma(10),
            dma(3),
            pltpu.SemaphoreType.DMA,
            pltpu.SemaphoreType.DMA,
            dma(10),
            dma(10),
            dma(10),
        ],
        compiler_params=pltpu.CompilerParams(
            collective_id=0, has_side_effects=True, vmem_limit_bytes=52 << 20
        ),
    )(start_state.reshape(flat), node_offset.reshape(flat))
    return out.reshape((1,) + start_state.shape)


def solution(mesh):
    return jax.shard_map(
        body,
        mesh=mesh,
        in_specs=(
            P(None, None, None, None, "space", None),
            P("node", None, None, None, None, "space", None),
        ),
        out_specs=P("node", None, None, None, None, "space", None),
        check_vma=False,
    )
```

```python
import functools
import math

import jax
import jax.numpy as jnp
import numpy as np
from jax import lax
from jax.experimental import pallas as pl
from jax.experimental.pallas import tpu as pltpu
from jax.sharding import PartitionSpec as P

MESH = pl.DeviceIdType.MESH
TILES = 10
GAS = 1.4
STEP = 0.01


def lobatto_derivative():
    points = np.array([-1.0, -math.sqrt(0.2), math.sqrt(0.2), 1.0])
    barycentric = np.ones(4)
    for i in range(4):
        for k in range(4):
            if k != i:
                barycentric[i] = barycentric[i] / (points[i] - points[k])
    derivative = np.zeros((4, 4))
    for i in range(4):
        for j in range(4):
            if i != j:
                derivative[i, j] = barycentric[j] / barycentric[i] / (points[i] - points[j])
        derivative[i, i] = -np.sum(derivative[i])
    return derivative


def collocation_matrix():
    near_root = math.sqrt(3.0 / 7 - 2.0 / 7 * math.sqrt(1.2))
    far_root = math.sqrt(3.0 / 7 + 2.0 / 7 * math.sqrt(1.2))
    time_nodes = [(1.0 + value) / 2 for value in (-far_root, -near_root, near_root, far_root)]
    quad_table = np.zeros((4, 4))
    for j in range(4):
        coeffs = [1.0]
        for k in range(4):
            if k != j:
                scale = 1.0 / (time_nodes[j] - time_nodes[k])
                widened = [0.0] * (len(coeffs) + 1)
                for power in range(len(coeffs)):
                    widened[power + 1] = widened[power + 1] + coeffs[power] * scale
                    widened[power] = widened[power] - time_nodes[k] * coeffs[power] * scale
                coeffs = widened
        for m in range(4):
            total = 0.0
            for power in range(len(coeffs)):
                total = total + coeffs[power] * time_nodes[m] ** (power + 1) / (power + 1)
            quad_table[m, j] = total
    return quad_table


D = [[float(value) for value in row] for row in lobatto_derivative()]
Q = [[float(STEP * value) for value in row] for row in collocation_matrix()]


def lanes():
    return lax.broadcasted_iota(jnp.int32, (8, 128), 1)


def upper_half():
    return lax.broadcasted_iota(jnp.int32, (8, 128), 0) < 4


def swap(value):
    return pltpu.roll(value, 4, 0)


def turn(value, shift):
    return pltpu.roll(value, shift, 1)


def primitives(state, direction):
    inverse = 1.0 / state[0]
    speeds = [state[1 + k] * inverse for k in range(3)]
    kinetic = state[1] * speeds[0] + state[2] * speeds[1] + state[3] * speeds[2]
    pressure = (GAS - 1.0) * (state[4] - 0.5 * kinetic)
    return inverse, speeds[direction], pressure


def fluxes(state, speed, pressure, direction):
    columns = [state[1 + direction]]
    for k in range(3):
        entry = state[1 + k] * speed
        columns.append(entry + pressure if k == direction else entry)
    columns.append((state[4] + pressure) * speed)
    return columns


def wave(inverse, speed, pressure):
    return jnp.abs(speed) + jnp.sqrt(GAS * pressure * inverse)


def lift(own, own_flux, own_wave, other, direction, sign):
    inverse, speed, pressure = primitives(other, direction)
    other_flux = fluxes(other, speed, pressure, direction)
    top = jnp.maximum(own_wave, wave(inverse, speed, pressure))
    return [
        3.0 * (sign * (other_flux[v] - own_flux[v]) + top * (other[v] - own[v])) for v in range(5)
    ]


def derivative(values):
    out = []
    for i in range(4):
        row = []
        for v in range(5):
            total = None
            for j in range(4):
                if abs(D[i][j]) > 1e-12:
                    term = (-D[i][j]) * values[j][v]
                    total = term if total is None else total + term
            row.append(total)
        out.append(row)
    return out


def strided(ref, at, v, pair, c):
    return ref[at, v, pl.ds(32 * pair + c, 8, 4), :]


def rows(ref, at, v, start):
    return ref[at, v, pl.ds(start, 8), :]


def pass_z(u, at, before, after, out, to, tile):
    lane = lanes()
    base = lax.rem(48 * tile, 80)
    place = lane + base
    first = (place == 0) | (place == 80) | (place == 160)
    last = (place == 79) | (place == 159)
    for pair in range(2):
        state = [[strided(u, at, v, pair, c) for v in range(5)] for c in range(4)]
        prims = [primitives(state[c], 2) for c in range(4)]
        flux = [fluxes(state[c], prims[c][1], prims[c][2], 2) for c in range(4)]
        rate = derivative(flux)
        left = []
        right = []
        for v in range(5):
            back = strided(u, before, v, pair, 3)
            ahead = strided(u, after, v, pair, 3)
            near = turn(jnp.where(lane == 127, back, state[3][v]), 1)
            far = turn(jnp.where(lane >= 79, state[3][v], ahead), 49)
            left.append(jnp.where(first, far, near))
            back = strided(u, before, v, pair, 0)
            ahead = strided(u, after, v, pair, 0)
            near = turn(jnp.where(lane == 0, ahead, state[0][v]), 127)
            far = turn(jnp.where(lane >= 49, back, state[0][v]), 79)
            right.append(jnp.where(last, far, near))
        low = lift(state[0], flux[0], wave(*prims[0]), left, 2, 1.0)
        high = lift(state[3], flux[3], wave(*prims[3]), right, 2, -1.0)
        for v in range(5):
            for c in range(4):
                value = rate[c][v]
                if c == 0:
                    value = value + low[v]
                if c == 3:
                    value = value + high[v]
                out[to, v, pl.ds(32 * pair + c, 8, 4), :] = value


def pass_y(u, at, before, after, out, to):
    lane = lanes()
    half = upper_half()
    sign = jnp.where(half, 1.0, -1.0).astype(jnp.float32)

    def two(x, y):
        return jnp.where(half, jnp.float32(-x), jnp.float32(-y))

    mix_low = [two(D[0][0], D[1][1]), two(D[0][1], D[1][0]), two(D[0][2], D[1][3]), two(D[0][3], D[1][2])]
    mix_high = [two(D[2][0], D[3][1]), two(D[2][1], D[3][0]), two(D[2][2], D[3][3]), two(D[2][3], D[3][2])]
    for a in range(4):
        low = [rows(u, at, v, 16 * a) for v in range(5)]
        high = [rows(u, at, v, 16 * a + 8) for v in range(5)]
        prim_low = primitives(low, 1)
        prim_high = primitives(high, 1)
        flux_low = fluxes(low, prim_low[1], prim_low[2], 1)
        flux_high = fluxes(high, prim_high[1], prim_high[2], 1)
        own = [jnp.where(half, low[v], high[v]) for v in range(5)]
        own_flux = [jnp.where(half, flux_low[v], flux_high[v]) for v in range(5)]
        own_wave = wave(*[jnp.where(half, x, y) for x, y in zip(prim_low, prim_high)])
        other = []
        for v in range(5):
            back = rows(u, before, v, 16 * a + 8)
            ahead = rows(u, after, v, 16 * a)
            down = turn(jnp.where(lane >= 48, back, high[v]), 80)
            up = turn(jnp.where(lane >= 80, low[v], ahead), 48)
            other.append(swap(jnp.where(half, up, down)))
        face = lift(own, own_flux, own_wave, other, 1, sign)
        for v in range(5):
            parts = [flux_low[v], swap(flux_low[v]), flux_high[v], swap(flux_high[v])]
            sum_low = jnp.where(half, face[v], 0.0)
            sum_high = jnp.where(half, 0.0, face[v])
            for k in range(4):
                sum_low = sum_low + mix_low[k] * parts[k]
                sum_high = sum_high + mix_high[k] * parts[k]
            out[to, v, pl.ds(16 * a, 8), :] += sum_low
            out[to, v, pl.ds(16 * a + 8, 8), :] += sum_high


def pass_x(u, at, out, to):
    for h in range(2):
        state = [[rows(u, at, v, 16 * a + 8 * h) for v in range(5)] for a in range(4)]
        flux = []
        for a in range(4):
            _, speed, pressure = primitives(state[a], 0)
            flux.append(fluxes(state[a], speed, pressure, 0))
        rate = derivative(flux)
        for a in range(4):
            for v in range(5):
                out[to, v, pl.ds(16 * a + 8 * h, 8), :] += rate[a][v]


def faces_x(u, at, lower, low_at, upper, up_at, out, to):
    for h in range(2):
        for a, other, sign in ((0, lower, 1.0), (3, upper, -1.0)):
            own = [rows(u, at, v, 16 * a + 8 * h) for v in range(5)]
            inverse, speed, pressure = primitives(own, 0)
            own_flux = fluxes(own, speed, pressure, 0)
            trace = [other(v, h) for v in range(5)]
            face = lift(own, own_flux, wave(inverse, speed, pressure), trace, 0, sign)
            for v in range(5):
                out[to, v, pl.ds(16 * a + 8 * h, 8), :] += face[v]


def inner_rate(u, at, before, after, out, to, tile):
    pass_z(u, at, before, after, out, to, tile)
    pass_y(u, at, before, after, out, to)
    pass_x(u, at, out, to)


def pack(ref, at, side, tile):
    lane = lanes()
    half = upper_half()
    packed = []
    for v in range(5):
        for pair in range(2):
            if side == 0:
                one = rows(ref, at, v, 32 * pair + 8)
                two = rows(ref, at, v, 32 * pair + 24)
                main = jnp.where(half, swap(one), two)
            else:
                one = rows(ref, at, v, 32 * pair)
                two = rows(ref, at, v, 32 * pair + 16)
                main = jnp.where(half, one, swap(two))
            if tile is not None:
                c0 = strided(ref, at, v, pair, 0)
                c3 = strided(ref, at, v, pair, 3)
                if side == 0:
                    main = jnp.where(lane == 0, turn(c0, 8 + 8 * tile), main)
                    main = jnp.where(lane == 1, turn(c3, 2), main)
                else:
                    main = jnp.where(lane == 127, turn(c0, 127), main)
                    main = jnp.where(lane == 126, turn(c3, 47 + 8 * tile), main)
            packed.append(main)
    return packed


def unpack(packed, ref, at, side, columns):
    for v in range(5):
        for pair in range(2):
            block = packed[2 * v + pair]
            if columns:
                at0, at3 = (0, 1) if side == 0 else (127, 126)
                c0 = jnp.broadcast_to(block[:, at0 : at0 + 1], (8, 128))
                c3 = jnp.broadcast_to(block[:, at3 : at3 + 1], (8, 128))
                ref[at, v, pl.ds(32 * pair, 8, 4), :] = c0
                ref[at, v, pl.ds(32 * pair + 3, 8, 4), :] = c3
            shift = 12 if side == 0 else 0
            ref[at, v, pl.ds(32 * pair + shift, 4), :] = block[0:4]
            ref[at, v, pl.ds(32 * pair + 16 + shift, 4), :] = block[4:8]


def squeeze(packed, side):
    lane = lanes()
    blocks = [turn(block, 80) for block in packed] if side == 0 else packed
    full = [jnp.where(lane < 64, blocks[2 * i], turn(blocks[2 * i + 1], 64)) for i in range(5)]
    for group in (range(8), range(8, 10)):
        tail = turn(blocks[group[0]], 64)
        for g, k in enumerate(group):
            if g:
                tail = jnp.where(lane >= 16 * g, turn(blocks[k], (64 + 16 * g) % 128), tail)
        full.append(tail)
    return full


def stretch(full, side):
    lane = lanes()
    packed = []
    for k in range(10):
        main = full[k // 2]
        if k % 2:
            main = turn(main, 64)
        tail = full[5 + k // 8]
        shift = (64 - 16 * (k % 8)) % 128
        if shift:
            tail = turn(tail, shift)
        block = jnp.where(lane < 64, main, tail)
        packed.append(turn(block, 48) if side == 0 else block)
    return packed


MID_FIRST = 3
HELPER = -2
ONWARD = 1 - HELPER


def relayed(t):
    return (t == 1) | (t == 2) | (t == 3) | (t == 7) | (t == 8) | (t == 6)


def kernel(
    start_hbm,
    offset_hbm,
    out_hbm,
    start,
    u0,
    x_low,
    x_high,
    rate,
    halo_send,
    landed,
    halo,
    u1,
    x_low2,
    x_high2,
    rate2,
    give,
    pair_send,
    pair_land,
    relay,
    load_sem,
    x_send,
    x_recv,
    mid_send,
    mid_recv,
    end_send,
    end_recv,
    halo_ssem,
    halo_rsem,
    own_sem,
    own_halo_sem,
    x_send2,
    x_recv2,
    give_send,
    give_recv,
    give_own,
    pair_ssem,
    pair_rsem,
    relay_send,
    relay_recv,
    onward_send,
):
    m = lax.axis_index("node")
    s = lax.axis_index("space")
    hi = (s // 8) % 2
    q = m + hi * (3 - 2 * m)
    odd = q % 2
    left = 1 - q // 2
    up = (s + 1) % 64
    down = (s + 63) % 64
    hi_up = (up // 8) % 2
    hi_down = (down // 8) % 2
    q_up = q + hi_up * (3 - 2 * q)
    q_down = q + hi_down * (3 - 2 * q)
    slot_from = (3 - q) // 3
    slot_to = 3 - q // 3
    first_tile = 3 * q - 1
    k_from = 1 - (q % 3 + 1) // 2
    other_q = q + 1 - 2 * odd
    partner = other_q + hi * (3 - 2 * other_q)
    far_up = s % 8 == 7
    far_down = s % 8 == 0
    helps_up = s % 8 == (7 + HELPER) % 8
    helps_down = s % 8 == (-HELPER) % 8

    def space(distance):
        return (s + 64 + distance) % 64

    def turn_of(i):
        g = i % 5
        near = (g % 2) * ((g - 1) // 2) + (1 - g % 2) * (4 - g // 2)
        flip = (i // 5 + left) % 2
        return near + flip * (9 - 2 * near)

    def place_of(d):
        return d + hi * (3 - 2 * d)

    def loads(t):
        return (
            pltpu.make_async_copy(start_hbm.at[:, :, t, 0, :], start.at[t], load_sem.at[0, t]),
            pltpu.make_async_copy(offset_hbm.at[:, :, t, 0, :], u0.at[t], load_sem.at[1, t]),
        )

    def begin(i, carry):
        one, two = loads(turn_of(i))
        one.start()
        two.start()
        return carry

    lax.fori_loop(0, TILES, begin, 0)

    barrier = pltpu.get_barrier_semaphore()
    for k in range(1, 4):
        pl.semaphore_signal(barrier, inc=1, device_id={"node": (m + k) % 4}, device_id_type=MESH)
    pl.semaphore_signal(barrier, inc=1, device_id={"space": up}, device_id_type=MESH)
    pl.semaphore_signal(barrier, inc=1, device_id={"space": down}, device_id_type=MESH)
    pl.semaphore_signal(barrier, inc=1, device_id={"node": q_up, "space": up}, device_id_type=MESH)
    pl.semaphore_signal(barrier, inc=1, device_id={"node": q_down, "space": down}, device_id_type=MESH)
    for role, friends in (
        (far_up, (HELPER, 1 - HELPER)),
        (far_down, (-HELPER, HELPER - 1)),
        (helps_up, (-HELPER, ONWARD)),
        (helps_down, (HELPER, -ONWARD)),
    ):

        @pl.when(role)
        def _(friends=friends):
            for friend in friends:
                pl.semaphore_signal(
                    barrier, inc=1, device_id={"space": space(friend)}, device_id_type=MESH
                )

    in_relay = far_up | far_down | helps_up | helps_down

    @pl.when(in_relay)
    def _():
        pl.semaphore_wait(barrier, 9)

    @pl.when(jnp.logical_not(in_relay))
    def _():
        pl.semaphore_wait(barrier, 7)


    def x_copies(t):
        return (
            pltpu.make_async_remote_copy(
                src_ref=u0.at[t, :, pl.ds(48, 16)],
                dst_ref=x_low.at[t],
                send_sem=x_send.at[0, t],
                recv_sem=x_recv.at[0, t],
                device_id={"space": up},
                device_id_type=MESH,
            ),
            pltpu.make_async_remote_copy(
                src_ref=u0.at[t, :, pl.ds(0, 16)],
                dst_ref=x_high.at[t],
                send_sem=x_send.at[1, t],
                recv_sem=x_recv.at[1, t],
                device_id={"space": down},
                device_id_type=MESH,
            ),
        )

    def relay_copies(t):
        return (
            pltpu.make_async_remote_copy(
                src_ref=u0.at[t, :, pl.ds(48, 16)],
                dst_ref=relay.at[t],
                send_sem=relay_send.at[t],
                recv_sem=relay_recv.at[t],
                device_id={"space": space(HELPER)},
                device_id_type=MESH,
            ),
            pltpu.make_async_remote_copy(
                src_ref=u0.at[t, :, pl.ds(0, 16)],
                dst_ref=relay.at[t],
                send_sem=relay_send.at[t],
                recv_sem=relay_recv.at[t],
                device_id={"space": space(-HELPER)},
                device_id_type=MESH,
            ),
        )

    def onward_copies(t):
        return (
            pltpu.make_async_remote_copy(
                src_ref=relay.at[t],
                dst_ref=x_low.at[t],
                send_sem=onward_send.at[t],
                recv_sem=x_recv.at[0, t],
                device_id={"space": space(ONWARD)},
                device_id_type=MESH,
            ),
            pltpu.make_async_remote_copy(
                src_ref=relay.at[t],
                dst_ref=x_high.at[t],
                send_sem=onward_send.at[t],
                recv_sem=x_recv.at[1, t],
                device_id={"space": space(-ONWARD)},
                device_id_type=MESH,
            ),
        )

    def guess(i, carry):
        t = turn_of(i)
        one, two = loads(t)
        one.wait()
        two.wait()
        for v in range(5):
            u0[t, v] = u0[t, v] + start[t, v]
        one, two = x_copies(t)
        by_up, by_down = relay_copies(t)

        @pl.when(far_up & relayed(t))
        def _():
            by_up.start()

        @pl.when(jnp.logical_not(far_up & relayed(t)))
        def _():
            one.start()

        @pl.when(far_down & relayed(t))
        def _():
            by_down.start()

        @pl.when(jnp.logical_not(far_down & relayed(t)))
        def _():
            two.start()

        return carry

    lax.fori_loop(0, TILES, guess, 0)

    def owner(t):
        return (t + 1) // 3

    def mid_copy(t):
        d = owner(t)
        slot = t - 3 * d + 1
        return pltpu.make_async_remote_copy(
            src_ref=rate.at[t, :, pl.ds(16, 32)],
            dst_ref=landed.at[m, slot, :, pl.ds(16, 32)],
            send_sem=mid_send.at[t],
            recv_sem=mid_recv.at[m, slot],
            device_id={"node": place_of(d)},
            device_id_type=MESH,
        )

    def end_copies(t):
        d = owner(t)
        slot = t - 3 * d + 1
        return [
            pltpu.make_async_remote_copy(
                src_ref=rate.at[t, :, pl.ds(48 * k, 16)],
                dst_ref=landed.at[m, slot, :, pl.ds(48 * k, 16)],
                send_sem=end_send.at[k, t],
                recv_sem=end_recv.at[k, m, slot],
                device_id={"node": place_of(d)},
                device_id_type=MESH,
            )
            for k in range(2)
        ]

    def own_copy(slot):
        return pltpu.make_async_copy(
            rate.at[first_tile + slot], landed.at[m, slot], own_sem.at[slot]
        )

    def send_mid(i):
        t = turn_of(i)

        @pl.when(owner(t) != q)
        def _():
            mid_copy(t).start()

    def inside(i, carry):
        t = turn_of(i)
        inner_rate(u0, t, (t + 9) % 10, (t + 1) % 10, rate, t, t)

        @pl.when(i < MID_FIRST)
        def _():
            send_mid(i)

        return carry

    lax.fori_loop(0, TILES, inside, 0)

    def onward(t, carry):
        one, two = onward_copies(t)

        @pl.when(helps_up & relayed(t))
        def _():
            relay_copies(t)[0].wait_recv()
            one.start()

        @pl.when(helps_down & relayed(t))
        def _():
            relay_copies(t)[1].wait_recv()
            two.start()

        return carry

    lax.fori_loop(1, 9, onward, 0)

    def edges(i, carry):
        t = turn_of(i)
        one, two = x_copies(t)
        one.wait_recv()
        two.wait_recv()
        faces_x(
            u0,
            t,
            lambda v, h: x_low[t, v, pl.ds(8 * h, 8), :],
            t,
            lambda v, h: x_high[t, v, pl.ds(8 * h, 8), :],
            t,
            rate,
            t,
        )

        @pl.when(owner(t) != q)
        def _():
            for copy in end_copies(t):
                copy.start()

        @pl.when(owner(t) == q)
        def _():
            own_copy(t - first_tile).start()

        return carry

    lax.fori_loop(0, TILES, edges, 0)

    def halo_copy(d):
        return pltpu.make_async_remote_copy(
            src_ref=halo_send.at[d],
            dst_ref=halo.at[m],
            send_sem=halo_ssem.at[d],
            recv_sem=halo_rsem.at[m],
            device_id={"node": place_of(d)},
            device_id_type=MESH,
        )

    own_halo = pltpu.make_async_copy(halo_send.at[q], halo.at[m], own_halo_sem)

    for d, side, tile in ((0, 0, 9), (1, 1, 5), (2, 0, 4), (3, 1, 0)):
        for k, block in enumerate(squeeze(pack(rate, tile, side, None), side)):
            halo_send[d, pl.ds(8 * k, 8), :] = block

    def borders(d, carry):
        @pl.when(d != q)
        def _():
            halo_copy(d).start()

        return carry

    lax.fori_loop(0, 4, borders, 0)
    own_halo.start()

    def rest(i, carry):
        send_mid(i)
        return carry

    lax.fori_loop(MID_FIRST, TILES, rest, 0)

    def arrived(part, sem):
        pltpu.make_async_remote_copy(
            src_ref=part,
            dst_ref=part,
            send_sem=mid_send.at[0],
            recv_sem=sem,
            device_id={"node": (m + 1) % 4},
            device_id_type=MESH,
        ).wait_recv()

    def x_copies2(slot):
        return (
            pltpu.make_async_remote_copy(
                src_ref=u1.at[:, slot + 1, :, pl.ds(48, 16)],
                dst_ref=x_low2.at[slot],
                send_sem=x_send2.at[0, slot],
                recv_sem=x_recv2.at[0, slot],
                device_id={"node": q_up, "space": up},
                device_id_type=MESH,
            ),
            pltpu.make_async_remote_copy(
                src_ref=u1.at[:, slot + 1, :, pl.ds(0, 16)],
                dst_ref=x_high2.at[slot],
                send_sem=x_send2.at[1, slot],
                recv_sem=x_recv2.at[1, slot],
                device_id={"node": q_down, "space": down},
                device_id_type=MESH,
            ),
        )

    def advance(slot, offset, stride):
        def each(v, inner):
            for part in range(4):
                at = offset + 8 * (part % 2) + stride * (part // 2)
                held = [landed[j, slot, v, pl.ds(at, 8), :] for j in range(4)]
                base = start[first_tile + slot, v, pl.ds(at, 8), :]
                for k in range(4):
                    total = Q[k][0] * held[0]
                    for j in range(1, 4):
                        total = total + Q[k][j] * held[j]
                    u1[k, slot + 1, v, pl.ds(at, 8), :] = base + total
            return inner

        lax.fori_loop(0, 5, each, 0)

    def next_state(slot):
        def ends(j, carry):
            @pl.when(j != m)
            def _():
                for k in range(2):
                    arrived(landed.at[j, slot, :, pl.ds(48 * k, 16)], end_recv.at[k, j, slot])

            return carry

        own_copy(slot).wait()
        lax.fori_loop(0, 4, ends, 0)
        advance(slot, 0, 48)
        one, two = x_copies2(slot)
        one.start()
        two.start()

        def mids(j, carry):
            @pl.when(j != m)
            def _():
                arrived(landed.at[j, slot, :, pl.ds(16, 32)], mid_recv.at[j, slot])

            return carry

        lax.fori_loop(0, 4, mids, 0)
        advance(slot, 16, 16)

    def middle_rows():
        def wait(j, carry):
            @pl.when(j != m)
            def _():
                arrived(halo.at[j], halo_rsem.at[j])

            return carry

        own_halo.wait()
        lax.fori_loop(0, 4, wait, 0)

        def fill(side, tile, at):
            base = squeeze(pack(start, tile, side, None), side)
            held = [[halo[j, pl.ds(8 * k, 8), :] for k in range(7)] for j in range(4)]
            for node in range(4):
                blocks = []
                for k in range(7):
                    total = Q[node][0] * held[0][k]
                    for j in range(1, 4):
                        total = total + Q[node][j] * held[j][k]
                    blocks.append(base[k] + total)
                unpack(stretch(blocks, side), u1.at[node], at, side, False)

        @pl.when(odd == 0)
        def _():
            fill(0, (first_tile + slot_from + 9) % 10, slot_from)

        @pl.when(odd == 1)
        def _():
            fill(1, (first_tile + slot_to) % 10, slot_to + 1)

    pair_copy = pltpu.make_async_remote_copy(
        src_ref=pair_send,
        dst_ref=pair_land,
        send_sem=pair_ssem,
        recv_sem=pair_rsem,
        device_id={"node": partner},
        device_id_type=MESH,
    )

    def pair_out(slot):
        def give_rows(side):
            def each(node, carry):
                blocks = pack(u1.at[node], slot + 1, side, first_tile + slot)
                for k, block in enumerate(blocks):
                    pair_send[node, pl.ds(8 * k, 8), :] = block
                return carry

            lax.fori_loop(0, 4, each, 0)

        @pl.when(odd == 0)
        def _():
            give_rows(0)

        @pl.when(odd == 1)
        def _():
            give_rows(1)

        pair_copy.start()

    def pair_in():
        pair_copy.wait_recv()

        def take_rows(side, at):
            def each(node, carry):
                blocks = [pair_land[node, pl.ds(8 * k, 8), :] for k in range(10)]
                unpack(blocks, u1.at[node], at, side, True)
                return carry

            lax.fori_loop(0, 4, each, 0)

        @pl.when(odd == 0)
        def _():
            take_rows(1, slot_to + 1)

        @pl.when(odd == 1)
        def _():
            take_rows(0, slot_from)

    def give_copy(node, slot):
        return pltpu.make_async_remote_copy(
            src_ref=give.at[node, slot],
            dst_ref=out_hbm.at[:, :, first_tile + slot, 0, :],
            send_sem=give_send.at[node, slot],
            recv_sem=give_recv.at[first_tile + slot],
            device_id={"node": node},
            device_id_type=MESH,
        )

    def give_here(slot):
        return pltpu.make_async_copy(
            give.at[m, slot], out_hbm.at[:, :, first_tile + slot, 0, :], give_own.at[slot]
        )

    def second(slot):
        def each(node, carry):
            inner_rate(
                u1.at[node], slot + 1, slot, slot + 2, rate2.at[node], slot, first_tile + slot
            )
            return carry

        lax.fori_loop(0, 4, each, 0)
        one, two = x_copies2(slot)
        one.wait_recv()
        two.wait_recv()

        def edge(node, carry):
            faces_x(
                u1.at[node],
                slot + 1,
                lambda v, h: x_low2[slot, node, v, pl.ds(8 * h, 8), :],
                slot,
                lambda v, h: x_high2[slot, node, v, pl.ds(8 * h, 8), :],
                slot,
                rate2.at[node],
                slot,
            )
            return carry

        lax.fori_loop(0, 4, edge, 0)

        def gather(v, carry):
            for part in range(8):
                held = [rate2[j, slot, v, pl.ds(8 * part, 8), :] for j in range(4)]
                for k in range(4):
                    total = Q[k][0] * held[0]
                    for j in range(1, 4):
                        total = total + Q[k][j] * held[j]
                    give[k, slot, v, pl.ds(8 * part, 8), :] = total
            return carry

        lax.fori_loop(0, 5, gather, 0)

        def send(k, carry):
            node = (m + 2 + k) % 4

            @pl.when(node != m)
            def _():
                give_copy(node, slot).start()

            @pl.when(node == m)
            def _():
                give_here(slot).start()

            return carry

        lax.fori_loop(0, 4, send, 0)

    def slot_of(k):
        return k + odd * (2 - 2 * k)

    def stage(k, carry):
        @pl.when(k < 3)
        def _():
            next_state(slot_of(k))

        @pl.when(k == 2)
        def _():
            pair_out(slot_of(k))

        @pl.when(k == k_from + 1)
        def _():
            middle_rows()

        @pl.when(k == 3)
        def _():
            pair_in()

        @pl.when(k > k_from)
        def _():
            second(slot_of(k - 1))

        return carry

    lax.fori_loop(k_from, 4, stage, 0)

    def drain(t, carry):
        one, two = x_copies(t)
        by_up, by_down = relay_copies(t)
        on_up, on_down = onward_copies(t)

        @pl.when(far_up & relayed(t))
        def _():
            by_up.wait_send()

        @pl.when(jnp.logical_not(far_up & relayed(t)))
        def _():
            one.wait_send()

        @pl.when(far_down & relayed(t))
        def _():
            by_down.wait_send()

        @pl.when(jnp.logical_not(far_down & relayed(t)))
        def _():
            two.wait_send()

        @pl.when(helps_up & relayed(t))
        def _():
            on_up.wait_send()

        @pl.when(helps_down & relayed(t))
        def _():
            on_down.wait_send()

        @pl.when(owner(t) != q)
        def _():
            mid_copy(t).wait_send()
            for copy in end_copies(t):
                copy.wait_send()
            arrived(out_hbm.at[:, :, t, 0, :], give_recv.at[t])

        return carry

    lax.fori_loop(0, TILES, drain, 0)

    def drain_nodes(d, carry):
        @pl.when(d != q)
        def _():
            halo_copy(d).wait_send()

        return carry

    lax.fori_loop(0, 4, drain_nodes, 0)
    pair_copy.wait_send()

    def drain_slots(slot, carry):
        one, two = x_copies2(slot)
        one.wait_send()
        two.wait_send()
        give_here(slot).wait()

        def each(node, inner):
            @pl.when(node != m)
            def _():
                give_copy(node, slot).wait_send()

            return inner

        lax.fori_loop(0, 4, each, 0)
        return carry

    lax.fori_loop(slot_from, slot_to, drain_slots, 0)


def body(start_state, node_offset):
    flat = (5, 64, TILES, 1, 128)
    vmem = lambda *shape: pltpu.VMEM(shape, jnp.float32)
    dma = lambda *shape: pltpu.SemaphoreType.DMA(shape)
    out = pl.pallas_call(
        kernel,
        out_shape=jax.ShapeDtypeStruct(flat, jnp.float32),
        in_specs=[pl.BlockSpec(memory_space=pltpu.HBM)] * 2,
        out_specs=pl.BlockSpec(memory_space=pl.ANY),
        scratch_shapes=[
            vmem(10, 5, 64, 128),
            vmem(10, 5, 64, 128),
            vmem(10, 5, 16, 128),
            vmem(10, 5, 16, 128),
            vmem(10, 5, 64, 128),
            vmem(4, 56, 128),
            vmem(4, 3, 5, 64, 128),
            vmem(4, 56, 128),
            vmem(4, 5, 5, 64, 128),
            vmem(3, 4, 5, 16, 128),
            vmem(3, 4, 5, 16, 128),
            vmem(4, 3, 5, 64, 128),
            vmem(4, 3, 5, 64, 128),
            vmem(4, 80, 128),
            vmem(4, 80, 128),
            vmem(10, 5, 16, 128),
            dma(2, 10),
            dma(2, 10),
            dma(2, 10),
            dma(10),
            dma(4, 3),
            dma(2, 10),
            dma(2, 4, 3),
            dma(4),
            dma(4),
            dma(3),
            pltpu.SemaphoreType.DMA,
            dma(2, 3),
            dma(2, 3),
            dma(4, 3),
            dma(10),
            dma(3),
            pltpu.SemaphoreType.DMA,
            pltpu.SemaphoreType.DMA,
            dma(10),
            dma(10),
            dma(10),
        ],
        compiler_params=pltpu.CompilerParams(
            collective_id=0, has_side_effects=True, vmem_limit_bytes=52 << 20
        ),
    )(start_state.reshape(flat), node_offset.reshape(flat))
    return out.reshape((1,) + start_state.shape)


def solution(mesh):
    return jax.shard_map(
        body,
        mesh=mesh,
        in_specs=(
            P(None, None, None, None, "space", None),
            P("node", None, None, None, None, "space", None),
        ),
        out_specs=P("node", None, None, None, None, "space", None),
        check_vma=False,
    )
```

```python
import functools
import math

import jax
import jax.numpy as jnp
import numpy as np
from jax import lax
from jax.experimental import pallas as pl
from jax.experimental.pallas import tpu as pltpu
from jax.sharding import PartitionSpec as P

MESH = pl.DeviceIdType.MESH
TILES = 10
GAS = 1.4
STEP = 0.01


def lobatto_derivative():
    points = np.array([-1.0, -math.sqrt(0.2), math.sqrt(0.2), 1.0])
    barycentric = np.ones(4)
    for i in range(4):
        for k in range(4):
            if k != i:
                barycentric[i] = barycentric[i] / (points[i] - points[k])
    derivative = np.zeros((4, 4))
    for i in range(4):
        for j in range(4):
            if i != j:
                derivative[i, j] = barycentric[j] / barycentric[i] / (points[i] - points[j])
        derivative[i, i] = -np.sum(derivative[i])
    return derivative


def collocation_matrix():
    near_root = math.sqrt(3.0 / 7 - 2.0 / 7 * math.sqrt(1.2))
    far_root = math.sqrt(3.0 / 7 + 2.0 / 7 * math.sqrt(1.2))
    time_nodes = [(1.0 + value) / 2 for value in (-far_root, -near_root, near_root, far_root)]
    quad_table = np.zeros((4, 4))
    for j in range(4):
        coeffs = [1.0]
        for k in range(4):
            if k != j:
                scale = 1.0 / (time_nodes[j] - time_nodes[k])
                widened = [0.0] * (len(coeffs) + 1)
                for power in range(len(coeffs)):
                    widened[power + 1] = widened[power + 1] + coeffs[power] * scale
                    widened[power] = widened[power] - time_nodes[k] * coeffs[power] * scale
                coeffs = widened
        for m in range(4):
            total = 0.0
            for power in range(len(coeffs)):
                total = total + coeffs[power] * time_nodes[m] ** (power + 1) / (power + 1)
            quad_table[m, j] = total
    return quad_table


D = [[float(value) for value in row] for row in lobatto_derivative()]
Q = [[float(STEP * value) for value in row] for row in collocation_matrix()]


def lanes():
    return lax.broadcasted_iota(jnp.int32, (8, 128), 1)


def upper_half():
    return lax.broadcasted_iota(jnp.int32, (8, 128), 0) < 4


def swap(value):
    return pltpu.roll(value, 4, 0)


def turn(value, shift):
    return pltpu.roll(value, shift, 1)


def primitives(state, direction):
    inverse = 1.0 / state[0]
    speeds = [state[1 + k] * inverse for k in range(3)]
    kinetic = state[1] * speeds[0] + state[2] * speeds[1] + state[3] * speeds[2]
    pressure = (GAS - 1.0) * (state[4] - 0.5 * kinetic)
    return inverse, speeds[direction], pressure


def fluxes(state, speed, pressure, direction):
    columns = [state[1 + direction]]
    for k in range(3):
        entry = state[1 + k] * speed
        columns.append(entry + pressure if k == direction else entry)
    columns.append((state[4] + pressure) * speed)
    return columns


def wave(inverse, speed, pressure):
    return jnp.abs(speed) + jnp.sqrt(GAS * pressure * inverse)


def lift(own, own_flux, own_wave, other, direction, sign):
    inverse, speed, pressure = primitives(other, direction)
    other_flux = fluxes(other, speed, pressure, direction)
    top = jnp.maximum(own_wave, wave(inverse, speed, pressure))
    return [
        3.0 * (sign * (other_flux[v] - own_flux[v]) + top * (other[v] - own[v])) for v in range(5)
    ]


def derivative(values):
    out = []
    for i in range(4):
        row = []
        for v in range(5):
            total = None
            for j in range(4):
                if abs(D[i][j]) > 1e-12:
                    term = (-D[i][j]) * values[j][v]
                    total = term if total is None else total + term
            row.append(total)
        out.append(row)
    return out


def strided(ref, at, v, pair, c):
    return ref[at, v, pl.ds(32 * pair + c, 8, 4), :]


def rows(ref, at, v, start):
    return ref[at, v, pl.ds(start, 8), :]


def pass_z(u, at, before, after, out, to, tile):
    lane = lanes()
    base = lax.rem(48 * tile, 80)
    place = lane + base
    first = (place == 0) | (place == 80) | (place == 160)
    last = (place == 79) | (place == 159)
    for pair in range(2):
        state = [[strided(u, at, v, pair, c) for v in range(5)] for c in range(4)]
        prims = [primitives(state[c], 2) for c in range(4)]
        flux = [fluxes(state[c], prims[c][1], prims[c][2], 2) for c in range(4)]
        rate = derivative(flux)
        left = []
        right = []
        for v in range(5):
            back = strided(u, before, v, pair, 3)
            ahead = strided(u, after, v, pair, 3)
            near = turn(jnp.where(lane == 127, back, state[3][v]), 1)
            far = turn(jnp.where(lane >= 79, state[3][v], ahead), 49)
            left.append(jnp.where(first, far, near))
            back = strided(u, before, v, pair, 0)
            ahead = strided(u, after, v, pair, 0)
            near = turn(jnp.where(lane == 0, ahead, state[0][v]), 127)
            far = turn(jnp.where(lane >= 49, back, state[0][v]), 79)
            right.append(jnp.where(last, far, near))
        low = lift(state[0], flux[0], wave(*prims[0]), left, 2, 1.0)
        high = lift(state[3], flux[3], wave(*prims[3]), right, 2, -1.0)
        for v in range(5):
            for c in range(4):
                value = rate[c][v]
                if c == 0:
                    value = value + low[v]
                if c == 3:
                    value = value + high[v]
                out[to, v, pl.ds(32 * pair + c, 8, 4), :] = value


def pass_y(u, at, before, after, out, to):
    lane = lanes()
    half = upper_half()
    sign = jnp.where(half, 1.0, -1.0).astype(jnp.float32)

    def two(x, y):
        return jnp.where(half, jnp.float32(-x), jnp.float32(-y))

    mix_low = [two(D[0][0], D[1][1]), two(D[0][1], D[1][0]), two(D[0][2], D[1][3]), two(D[0][3], D[1][2])]
    mix_high = [two(D[2][0], D[3][1]), two(D[2][1], D[3][0]), two(D[2][2], D[3][3]), two(D[2][3], D[3][2])]
    for a in range(4):
        low = [rows(u, at, v, 16 * a) for v in range(5)]
        high = [rows(u, at, v, 16 * a + 8) for v in range(5)]
        prim_low = primitives(low, 1)
        prim_high = primitives(high, 1)
        flux_low = fluxes(low, prim_low[1], prim_low[2], 1)
        flux_high = fluxes(high, prim_high[1], prim_high[2], 1)
        own = [jnp.where(half, low[v], high[v]) for v in range(5)]
        own_flux = [jnp.where(half, flux_low[v], flux_high[v]) for v in range(5)]
        own_wave = wave(*[jnp.where(half, x, y) for x, y in zip(prim_low, prim_high)])
        other = []
        for v in range(5):
            back = rows(u, before, v, 16 * a + 8)
            ahead = rows(u, after, v, 16 * a)
            down = turn(jnp.where(lane >= 48, back, high[v]), 80)
            up = turn(jnp.where(lane >= 80, low[v], ahead), 48)
            other.append(swap(jnp.where(half, up, down)))
        face = lift(own, own_flux, own_wave, other, 1, sign)
        for v in range(5):
            parts = [flux_low[v], swap(flux_low[v]), flux_high[v], swap(flux_high[v])]
            sum_low = jnp.where(half, face[v], 0.0)
            sum_high = jnp.where(half, 0.0, face[v])
            for k in range(4):
                sum_low = sum_low + mix_low[k] * parts[k]
                sum_high = sum_high + mix_high[k] * parts[k]
            out[to, v, pl.ds(16 * a, 8), :] += sum_low
            out[to, v, pl.ds(16 * a + 8, 8), :] += sum_high


def pass_x(u, at, out, to):
    for h in range(2):
        state = [[rows(u, at, v, 16 * a + 8 * h) for v in range(5)] for a in range(4)]
        flux = []
        for a in range(4):
            _, speed, pressure = primitives(state[a], 0)
            flux.append(fluxes(state[a], speed, pressure, 0))
        rate = derivative(flux)
        for a in range(4):
            for v in range(5):
                out[to, v, pl.ds(16 * a + 8 * h, 8), :] += rate[a][v]


def faces_x(u, at, lower, low_at, upper, up_at, out, to):
    for h in range(2):
        for a, other, sign in ((0, lower, 1.0), (3, upper, -1.0)):
            own = [rows(u, at, v, 16 * a + 8 * h) for v in range(5)]
            inverse, speed, pressure = primitives(own, 0)
            own_flux = fluxes(own, speed, pressure, 0)
            trace = [other(v, h) for v in range(5)]
            face = lift(own, own_flux, wave(inverse, speed, pressure), trace, 0, sign)
            for v in range(5):
                out[to, v, pl.ds(16 * a + 8 * h, 8), :] += face[v]


def inner_rate(u, at, before, after, out, to, tile):
    pass_z(u, at, before, after, out, to, tile)
    pass_y(u, at, before, after, out, to)
    pass_x(u, at, out, to)


def pack(ref, at, side, tile):
    lane = lanes()
    half = upper_half()
    packed = []
    for v in range(5):
        for pair in range(2):
            if side == 0:
                one = rows(ref, at, v, 32 * pair + 8)
                two = rows(ref, at, v, 32 * pair + 24)
                main = jnp.where(half, swap(one), two)
            else:
                one = rows(ref, at, v, 32 * pair)
                two = rows(ref, at, v, 32 * pair + 16)
                main = jnp.where(half, one, swap(two))
            if tile is not None:
                c0 = strided(ref, at, v, pair, 0)
                c3 = strided(ref, at, v, pair, 3)
                if side == 0:
                    main = jnp.where(lane == 0, turn(c0, 8 + 8 * tile), main)
                    main = jnp.where(lane == 1, turn(c3, 2), main)
                else:
                    main = jnp.where(lane == 127, turn(c0, 127), main)
                    main = jnp.where(lane == 126, turn(c3, 47 + 8 * tile), main)
            packed.append(main)
    return packed


def unpack(packed, ref, at, side, columns):
    for v in range(5):
        for pair in range(2):
            block = packed[2 * v + pair]
            if columns:
                at0, at3 = (0, 1) if side == 0 else (127, 126)
                c0 = jnp.broadcast_to(block[:, at0 : at0 + 1], (8, 128))
                c3 = jnp.broadcast_to(block[:, at3 : at3 + 1], (8, 128))
                ref[at, v, pl.ds(32 * pair, 8, 4), :] = c0
                ref[at, v, pl.ds(32 * pair + 3, 8, 4), :] = c3
            shift = 12 if side == 0 else 0
            ref[at, v, pl.ds(32 * pair + shift, 4), :] = block[0:4]
            ref[at, v, pl.ds(32 * pair + 16 + shift, 4), :] = block[4:8]


def squeeze(packed, side):
    lane = lanes()
    blocks = [turn(block, 80) for block in packed] if side == 0 else packed
    full = [jnp.where(lane < 64, blocks[2 * i], turn(blocks[2 * i + 1], 64)) for i in range(5)]
    for group in (range(8), range(8, 10)):
        tail = turn(blocks[group[0]], 64)
        for g, k in enumerate(group):
            if g:
                tail = jnp.where(lane >= 16 * g, turn(blocks[k], (64 + 16 * g) % 128), tail)
        full.append(tail)
    return full


def stretch(full, side):
    lane = lanes()
    packed = []
    for k in range(10):
        main = full[k // 2]
        if k % 2:
            main = turn(main, 64)
        tail = full[5 + k // 8]
        shift = (64 - 16 * (k % 8)) % 128
        if shift:
            tail = turn(tail, shift)
        block = jnp.where(lane < 64, main, tail)
        packed.append(turn(block, 48) if side == 0 else block)
    return packed


MID_FIRST = 3
HELPER = -2
ONWARD = 1 - HELPER


def relayed(t):
    return (t == 1) | (t == 2) | (t == 3) | (t == 7) | (t == 8) | (t == 6)


def kernel(
    start_hbm,
    offset_hbm,
    out_hbm,
    start,
    u0,
    x_low,
    x_high,
    rate,
    halo_send,
    landed,
    halo,
    u1,
    x_low2,
    x_high2,
    rate2,
    give,
    pair_send,
    pair_land,
    relay,
    load_sem,
    x_send,
    x_recv,
    mid_send,
    mid_recv,
    end_send,
    end_recv,
    halo_ssem,
    halo_rsem,
    own_sem,
    own_halo_sem,
    x_send2,
    x_recv2,
    give_send,
    give_recv,
    give_own,
    pair_ssem,
    pair_rsem,
    relay_send,
    relay_recv,
    onward_send,
):
    m = lax.axis_index("node")
    s = lax.axis_index("space")
    hi = (s // 8) % 2
    q = m + hi * (3 - 2 * m)
    odd = q % 2
    left = 1 - q // 2
    up = (s + 1) % 64
    down = (s + 63) % 64
    hi_up = (up // 8) % 2
    hi_down = (down // 8) % 2
    q_up = q + hi_up * (3 - 2 * q)
    q_down = q + hi_down * (3 - 2 * q)
    slot_from = (3 - q) // 3
    slot_to = 3 - q // 3
    first_tile = 3 * q - 1
    k_from = 1 - (q % 3 + 1) // 2
    other_q = q + 1 - 2 * odd
    partner = other_q + hi * (3 - 2 * other_q)
    far_up = s % 8 == 7
    far_down = s % 8 == 0
    helps_up = s % 8 == (7 + HELPER) % 8
    helps_down = s % 8 == (-HELPER) % 8

    def space(distance):
        return (s + 64 + distance) % 64

    def turn_of(i):
        g = i % 5
        near = (g % 2) * ((g - 1) // 2) + (1 - g % 2) * (4 - g // 2)
        flip = (i // 5 + left) % 2
        return near + flip * (9 - 2 * near)

    def place_of(d):
        return d + hi * (3 - 2 * d)

    def loads(t):
        return (
            pltpu.make_async_copy(start_hbm.at[:, :, t, 0, :], start.at[t], load_sem.at[0, t]),
            pltpu.make_async_copy(offset_hbm.at[:, :, t, 0, :], u0.at[t], load_sem.at[1, t]),
        )

    def begin(i, carry):
        one, two = loads(turn_of(i))
        one.start()
        two.start()
        return carry

    lax.fori_loop(0, TILES, begin, 0)

    barrier = pltpu.get_barrier_semaphore()
    for k in range(1, 4):
        pl.semaphore_signal(barrier, inc=1, device_id={"node": (m + k) % 4}, device_id_type=MESH)
    pl.semaphore_signal(barrier, inc=1, device_id={"space": up}, device_id_type=MESH)
    pl.semaphore_signal(barrier, inc=1, device_id={"space": down}, device_id_type=MESH)
    pl.semaphore_signal(barrier, inc=1, device_id={"node": q_up, "space": up}, device_id_type=MESH)
    pl.semaphore_signal(barrier, inc=1, device_id={"node": q_down, "space": down}, device_id_type=MESH)
    for role, friends in (
        (far_up, (HELPER, 1 - HELPER)),
        (far_down, (-HELPER, HELPER - 1)),
        (helps_up, (-HELPER, ONWARD)),
        (helps_down, (HELPER, -ONWARD)),
    ):

        @pl.when(role)
        def _(friends=friends):
            for friend in friends:
                pl.semaphore_signal(
                    barrier, inc=1, device_id={"space": space(friend)}, device_id_type=MESH
                )

    in_relay = far_up | far_down | helps_up | helps_down

    @pl.when(in_relay)
    def _():
        pl.semaphore_wait(barrier, 9)

    @pl.when(jnp.logical_not(in_relay))
    def _():
        pl.semaphore_wait(barrier, 7)


    def x_copies(t):
        return (
            pltpu.make_async_remote_copy(
                src_ref=u0.at[t, :, pl.ds(48, 16)],
                dst_ref=x_low.at[t],
                send_sem=x_send.at[0, t],
                recv_sem=x_recv.at[0, t],
                device_id={"space": up},
                device_id_type=MESH,
            ),
            pltpu.make_async_remote_copy(
                src_ref=u0.at[t, :, pl.ds(0, 16)],
                dst_ref=x_high.at[t],
                send_sem=x_send.at[1, t],
                recv_sem=x_recv.at[1, t],
                device_id={"space": down},
                device_id_type=MESH,
            ),
        )

    def relay_copies(t):
        return (
            pltpu.make_async_remote_copy(
                src_ref=u0.at[t, :, pl.ds(48, 16)],
                dst_ref=relay.at[t],
                send_sem=relay_send.at[t],
                recv_sem=relay_recv.at[t],
                device_id={"space": space(HELPER)},
                device_id_type=MESH,
            ),
            pltpu.make_async_remote_copy(
                src_ref=u0.at[t, :, pl.ds(0, 16)],
                dst_ref=relay.at[t],
                send_sem=relay_send.at[t],
                recv_sem=relay_recv.at[t],
                device_id={"space": space(-HELPER)},
                device_id_type=MESH,
            ),
        )

    def onward_copies(t):
        return (
            pltpu.make_async_remote_copy(
                src_ref=relay.at[t],
                dst_ref=x_low.at[t],
                send_sem=onward_send.at[t],
                recv_sem=x_recv.at[0, t],
                device_id={"space": space(ONWARD)},
                device_id_type=MESH,
            ),
            pltpu.make_async_remote_copy(
                src_ref=relay.at[t],
                dst_ref=x_high.at[t],
                send_sem=onward_send.at[t],
                recv_sem=x_recv.at[1, t],
                device_id={"space": space(-ONWARD)},
                device_id_type=MESH,
            ),
        )

    def guess(i, carry):
        t = turn_of(i)
        one, two = loads(t)
        one.wait()
        two.wait()
        for v in range(5):
            u0[t, v] = u0[t, v] + start[t, v]
        one, two = x_copies(t)
        by_up, by_down = relay_copies(t)

        @pl.when(far_up & relayed(t))
        def _():
            by_up.start()

        @pl.when(jnp.logical_not(far_up & relayed(t)))
        def _():
            one.start()

        @pl.when(far_down & relayed(t))
        def _():
            by_down.start()

        @pl.when(jnp.logical_not(far_down & relayed(t)))
        def _():
            two.start()

        return carry

    lax.fori_loop(0, TILES, guess, 0)

    def owner(t):
        return (t + 1) // 3

    def mid_copy(t):
        d = owner(t)
        slot = t - 3 * d + 1
        return pltpu.make_async_remote_copy(
            src_ref=rate.at[t, :, pl.ds(16, 32)],
            dst_ref=landed.at[m, slot, :, pl.ds(16, 32)],
            send_sem=mid_send.at[t],
            recv_sem=mid_recv.at[m, slot],
            device_id={"node": place_of(d)},
            device_id_type=MESH,
        )

    def end_copies(t):
        d = owner(t)
        slot = t - 3 * d + 1
        return [
            pltpu.make_async_remote_copy(
                src_ref=rate.at[t, :, pl.ds(48 * k, 16)],
                dst_ref=landed.at[m, slot, :, pl.ds(48 * k, 16)],
                send_sem=end_send.at[k, t],
                recv_sem=end_recv.at[k, m, slot],
                device_id={"node": place_of(d)},
                device_id_type=MESH,
            )
            for k in range(2)
        ]

    def own_copy(slot):
        return pltpu.make_async_copy(
            rate.at[first_tile + slot], landed.at[m, slot], own_sem.at[slot]
        )

    def send_mid(i):
        t = turn_of(i)

        @pl.when(owner(t) != q)
        def _():
            mid_copy(t).start()

    def onward(t, carry):
        one, two = onward_copies(t)

        @pl.when(helps_up & relayed(t))
        def _():
            relay_copies(t)[0].wait_recv()
            one.start()

        @pl.when(helps_down & relayed(t))
        def _():
            relay_copies(t)[1].wait_recv()
            two.start()

        return carry

    def inside(i, carry):
        t = turn_of(i)
        inner_rate(u0, t, (t + 9) % 10, (t + 1) % 10, rate, t, t)

        @pl.when(i < MID_FIRST)
        def _():
            send_mid(i)

        @pl.when(i == 6)
        def _():
            lax.fori_loop(1, 9, onward, 0)

        return carry

    lax.fori_loop(0, TILES, inside, 0)


    def edges(i, carry):
        t = turn_of(i)
        one, two = x_copies(t)
        one.wait_recv()
        two.wait_recv()
        faces_x(
            u0,
            t,
            lambda v, h: x_low[t, v, pl.ds(8 * h, 8), :],
            t,
            lambda v, h: x_high[t, v, pl.ds(8 * h, 8), :],
            t,
            rate,
            t,
        )

        @pl.when(owner(t) != q)
        def _():
            for copy in end_copies(t):
                copy.start()

        @pl.when(owner(t) == q)
        def _():
            own_copy(t - first_tile).start()

        return carry

    lax.fori_loop(0, TILES, edges, 0)

    def halo_copy(d):
        return pltpu.make_async_remote_copy(
            src_ref=halo_send.at[d],
            dst_ref=halo.at[m],
            send_sem=halo_ssem.at[d],
            recv_sem=halo_rsem.at[m],
            device_id={"node": place_of(d)},
            device_id_type=MESH,
        )

    own_halo = pltpu.make_async_copy(halo_send.at[q], halo.at[m], own_halo_sem)

    for d, side, tile in ((0, 0, 9), (1, 1, 5), (2, 0, 4), (3, 1, 0)):
        for k, block in enumerate(squeeze(pack(rate, tile, side, None), side)):
            halo_send[d, pl.ds(8 * k, 8), :] = block

    def borders(d, carry):
        @pl.when(d != q)
        def _():
            halo_copy(d).start()

        return carry

    lax.fori_loop(0, 4, borders, 0)
    own_halo.start()

    def rest(i, carry):
        send_mid(i)
        return carry

    lax.fori_loop(MID_FIRST, TILES, rest, 0)

    def arrived(part, sem):
        pltpu.make_async_remote_copy(
            src_ref=part,
            dst_ref=part,
            send_sem=mid_send.at[0],
            recv_sem=sem,
            device_id={"node": (m + 1) % 4},
            device_id_type=MESH,
        ).wait_recv()

    def x_copies2(slot):
        return (
            pltpu.make_async_remote_copy(
                src_ref=u1.at[:, slot + 1, :, pl.ds(48, 16)],
                dst_ref=x_low2.at[slot],
                send_sem=x_send2.at[0, slot],
                recv_sem=x_recv2.at[0, slot],
                device_id={"node": q_up, "space": up},
                device_id_type=MESH,
            ),
            pltpu.make_async_remote_copy(
                src_ref=u1.at[:, slot + 1, :, pl.ds(0, 16)],
                dst_ref=x_high2.at[slot],
                send_sem=x_send2.at[1, slot],
                recv_sem=x_recv2.at[1, slot],
                device_id={"node": q_down, "space": down},
                device_id_type=MESH,
            ),
        )

    def advance(slot, offset, stride):
        def each(v, inner):
            for part in range(4):
                at = offset + 8 * (part % 2) + stride * (part // 2)
                held = [landed[j, slot, v, pl.ds(at, 8), :] for j in range(4)]
                base = start[first_tile + slot, v, pl.ds(at, 8), :]
                for k in range(4):
                    total = Q[k][0] * held[0]
                    for j in range(1, 4):
                        total = total + Q[k][j] * held[j]
                    u1[k, slot + 1, v, pl.ds(at, 8), :] = base + total
            return inner

        lax.fori_loop(0, 5, each, 0)

    def next_state(slot):
        def ends(j, carry):
            @pl.when(j != m)
            def _():
                for k in range(2):
                    arrived(landed.at[j, slot, :, pl.ds(48 * k, 16)], end_recv.at[k, j, slot])

            return carry

        own_copy(slot).wait()
        lax.fori_loop(0, 4, ends, 0)
        advance(slot, 0, 48)
        one, two = x_copies2(slot)
        one.start()
        two.start()

        def mids(j, carry):
            @pl.when(j != m)
            def _():
                arrived(landed.at[j, slot, :, pl.ds(16, 32)], mid_recv.at[j, slot])

            return carry

        lax.fori_loop(0, 4, mids, 0)
        advance(slot, 16, 16)

    def middle_rows():
        def wait(j, carry):
            @pl.when(j != m)
            def _():
                arrived(halo.at[j], halo_rsem.at[j])

            return carry

        own_halo.wait()
        lax.fori_loop(0, 4, wait, 0)

        def fill(side, tile, at):
            base = squeeze(pack(start, tile, side, None), side)
            held = [[halo[j, pl.ds(8 * k, 8), :] for k in range(7)] for j in range(4)]
            for node in range(4):
                blocks = []
                for k in range(7):
                    total = Q[node][0] * held[0][k]
                    for j in range(1, 4):
                        total = total + Q[node][j] * held[j][k]
                    blocks.append(base[k] + total)
                unpack(stretch(blocks, side), u1.at[node], at, side, False)

        @pl.when(odd == 0)
        def _():
            fill(0, (first_tile + slot_from + 9) % 10, slot_from)

        @pl.when(odd == 1)
        def _():
            fill(1, (first_tile + slot_to) % 10, slot_to + 1)

    pair_copy = pltpu.make_async_remote_copy(
        src_ref=pair_send,
        dst_ref=pair_land,
        send_sem=pair_ssem,
        recv_sem=pair_rsem,
        device_id={"node": partner},
        device_id_type=MESH,
    )

    def pair_out(slot):
        def give_rows(side):
            def each(node, carry):
                blocks = pack(u1.at[node], slot + 1, side, first_tile + slot)
                for k, block in enumerate(blocks):
                    pair_send[node, pl.ds(8 * k, 8), :] = block
                return carry

            lax.fori_loop(0, 4, each, 0)

        @pl.when(odd == 0)
        def _():
            give_rows(0)

        @pl.when(odd == 1)
        def _():
            give_rows(1)

        pair_copy.start()

    def pair_in():
        pair_copy.wait_recv()

        def take_rows(side, at):
            def each(node, carry):
                blocks = [pair_land[node, pl.ds(8 * k, 8), :] for k in range(10)]
                unpack(blocks, u1.at[node], at, side, True)
                return carry

            lax.fori_loop(0, 4, each, 0)

        @pl.when(odd == 0)
        def _():
            take_rows(1, slot_to + 1)

        @pl.when(odd == 1)
        def _():
            take_rows(0, slot_from)

    def give_copy(node, slot):
        return pltpu.make_async_remote_copy(
            src_ref=give.at[node, slot],
            dst_ref=out_hbm.at[:, :, first_tile + slot, 0, :],
            send_sem=give_send.at[node, slot],
            recv_sem=give_recv.at[first_tile + slot],
            device_id={"node": node},
            device_id_type=MESH,
        )

    def give_here(slot):
        return pltpu.make_async_copy(
            give.at[m, slot], out_hbm.at[:, :, first_tile + slot, 0, :], give_own.at[slot]
        )

    def second(slot):
        def each(node, carry):
            inner_rate(
                u1.at[node], slot + 1, slot, slot + 2, rate2.at[node], slot, first_tile + slot
            )
            return carry

        lax.fori_loop(0, 4, each, 0)
        one, two = x_copies2(slot)
        one.wait_recv()
        two.wait_recv()

        def edge(node, carry):
            faces_x(
                u1.at[node],
                slot + 1,
                lambda v, h: x_low2[slot, node, v, pl.ds(8 * h, 8), :],
                slot,
                lambda v, h: x_high2[slot, node, v, pl.ds(8 * h, 8), :],
                slot,
                rate2.at[node],
                slot,
            )
            return carry

        lax.fori_loop(0, 4, edge, 0)

        def gather(v, carry):
            for part in range(8):
                held = [rate2[j, slot, v, pl.ds(8 * part, 8), :] for j in range(4)]
                for k in range(4):
                    total = Q[k][0] * held[0]
                    for j in range(1, 4):
                        total = total + Q[k][j] * held[j]
                    give[k, slot, v, pl.ds(8 * part, 8), :] = total
            return carry

        lax.fori_loop(0, 5, gather, 0)

        def send(k, carry):
            node = (m + 2 + k) % 4

            @pl.when(node != m)
            def _():
                give_copy(node, slot).start()

            @pl.when(node == m)
            def _():
                give_here(slot).start()

            return carry

        lax.fori_loop(0, 4, send, 0)

    def slot_of(k):
        return k + odd * (2 - 2 * k)

    def stage(k, carry):
        @pl.when(k < 3)
        def _():
            next_state(slot_of(k))

        @pl.when(k == 2)
        def _():
            pair_out(slot_of(k))

        @pl.when(k == k_from + 1)
        def _():
            middle_rows()

        @pl.when(k == 3)
        def _():
            pair_in()

        @pl.when(k > k_from)
        def _():
            second(slot_of(k - 1))

        return carry

    lax.fori_loop(k_from, 4, stage, 0)

    def drain(t, carry):
        one, two = x_copies(t)
        by_up, by_down = relay_copies(t)
        on_up, on_down = onward_copies(t)

        @pl.when(far_up & relayed(t))
        def _():
            by_up.wait_send()

        @pl.when(jnp.logical_not(far_up & relayed(t)))
        def _():
            one.wait_send()

        @pl.when(far_down & relayed(t))
        def _():
            by_down.wait_send()

        @pl.when(jnp.logical_not(far_down & relayed(t)))
        def _():
            two.wait_send()

        @pl.when(helps_up & relayed(t))
        def _():
            on_up.wait_send()

        @pl.when(helps_down & relayed(t))
        def _():
            on_down.wait_send()

        @pl.when(owner(t) != q)
        def _():
            mid_copy(t).wait_send()
            for copy in end_copies(t):
                copy.wait_send()
            arrived(out_hbm.at[:, :, t, 0, :], give_recv.at[t])

        return carry

    lax.fori_loop(0, TILES, drain, 0)

    def drain_nodes(d, carry):
        @pl.when(d != q)
        def _():
            halo_copy(d).wait_send()

        return carry

    lax.fori_loop(0, 4, drain_nodes, 0)
    pair_copy.wait_send()

    def drain_slots(slot, carry):
        one, two = x_copies2(slot)
        one.wait_send()
        two.wait_send()
        give_here(slot).wait()

        def each(node, inner):
            @pl.when(node != m)
            def _():
                give_copy(node, slot).wait_send()

            return inner

        lax.fori_loop(0, 4, each, 0)
        return carry

    lax.fori_loop(slot_from, slot_to, drain_slots, 0)


def body(start_state, node_offset):
    flat = (5, 64, TILES, 1, 128)
    vmem = lambda *shape: pltpu.VMEM(shape, jnp.float32)
    dma = lambda *shape: pltpu.SemaphoreType.DMA(shape)
    out = pl.pallas_call(
        kernel,
        out_shape=jax.ShapeDtypeStruct(flat, jnp.float32),
        in_specs=[pl.BlockSpec(memory_space=pltpu.HBM)] * 2,
        out_specs=pl.BlockSpec(memory_space=pl.ANY),
        scratch_shapes=[
            vmem(10, 5, 64, 128),
            vmem(10, 5, 64, 128),
            vmem(10, 5, 16, 128),
            vmem(10, 5, 16, 128),
            vmem(10, 5, 64, 128),
            vmem(4, 56, 128),
            vmem(4, 3, 5, 64, 128),
            vmem(4, 56, 128),
            vmem(4, 5, 5, 64, 128),
            vmem(3, 4, 5, 16, 128),
            vmem(3, 4, 5, 16, 128),
            vmem(4, 3, 5, 64, 128),
            vmem(4, 3, 5, 64, 128),
            vmem(4, 80, 128),
            vmem(4, 80, 128),
            vmem(10, 5, 16, 128),
            dma(2, 10),
            dma(2, 10),
            dma(2, 10),
            dma(10),
            dma(4, 3),
            dma(2, 10),
            dma(2, 4, 3),
            dma(4),
            dma(4),
            dma(3),
            pltpu.SemaphoreType.DMA,
            dma(2, 3),
            dma(2, 3),
            dma(4, 3),
            dma(10),
            dma(3),
            pltpu.SemaphoreType.DMA,
            pltpu.SemaphoreType.DMA,
            dma(10),
            dma(10),
            dma(10),
        ],
        compiler_params=pltpu.CompilerParams(
            collective_id=0, has_side_effects=True, vmem_limit_bytes=52 << 20
        ),
    )(start_state.reshape(flat), node_offset.reshape(flat))
    return out.reshape((1,) + start_state.shape)


def solution(mesh):
    return jax.shard_map(
        body,
        mesh=mesh,
        in_specs=(
            P(None, None, None, None, "space", None),
            P("node", None, None, None, None, "space", None),
        ),
        out_specs=P("node", None, None, None, None, "space", None),
        check_vma=False,
    )
```

```python
import functools
import math

import jax
import jax.numpy as jnp
import numpy as np
from jax import lax
from jax.experimental import pallas as pl
from jax.experimental.pallas import tpu as pltpu
from jax.sharding import PartitionSpec as P

MESH = pl.DeviceIdType.MESH
TILES = 10
GAS = 1.4
STEP = 0.01


def lobatto_derivative():
    points = np.array([-1.0, -math.sqrt(0.2), math.sqrt(0.2), 1.0])
    barycentric = np.ones(4)
    for i in range(4):
        for k in range(4):
            if k != i:
                barycentric[i] = barycentric[i] / (points[i] - points[k])
    derivative = np.zeros((4, 4))
    for i in range(4):
        for j in range(4):
            if i != j:
                derivative[i, j] = barycentric[j] / barycentric[i] / (points[i] - points[j])
        derivative[i, i] = -np.sum(derivative[i])
    return derivative


def collocation_matrix():
    near_root = math.sqrt(3.0 / 7 - 2.0 / 7 * math.sqrt(1.2))
    far_root = math.sqrt(3.0 / 7 + 2.0 / 7 * math.sqrt(1.2))
    time_nodes = [(1.0 + value) / 2 for value in (-far_root, -near_root, near_root, far_root)]
    quad_table = np.zeros((4, 4))
    for j in range(4):
        coeffs = [1.0]
        for k in range(4):
            if k != j:
                scale = 1.0 / (time_nodes[j] - time_nodes[k])
                widened = [0.0] * (len(coeffs) + 1)
                for power in range(len(coeffs)):
                    widened[power + 1] = widened[power + 1] + coeffs[power] * scale
                    widened[power] = widened[power] - time_nodes[k] * coeffs[power] * scale
                coeffs = widened
        for m in range(4):
            total = 0.0
            for power in range(len(coeffs)):
                total = total + coeffs[power] * time_nodes[m] ** (power + 1) / (power + 1)
            quad_table[m, j] = total
    return quad_table


D = [[float(value) for value in row] for row in lobatto_derivative()]
Q = [[float(STEP * value) for value in row] for row in collocation_matrix()]


def lanes():
    return lax.broadcasted_iota(jnp.int32, (8, 128), 1)


def upper_half():
    return lax.broadcasted_iota(jnp.int32, (8, 128), 0) < 4


def swap(value):
    return pltpu.roll(value, 4, 0)


def turn(value, shift):
    return pltpu.roll(value, shift, 1)


def primitives(state, direction):
    inverse = 1.0 / state[0]
    speeds = [state[1 + k] * inverse for k in range(3)]
    kinetic = state[1] * speeds[0] + state[2] * speeds[1] + state[3] * speeds[2]
    pressure = (GAS - 1.0) * (state[4] - 0.5 * kinetic)
    return inverse, speeds[direction], pressure


def fluxes(state, speed, pressure, direction):
    columns = [state[1 + direction]]
    for k in range(3):
        entry = state[1 + k] * speed
        columns.append(entry + pressure if k == direction else entry)
    columns.append((state[4] + pressure) * speed)
    return columns


def wave(inverse, speed, pressure):
    return jnp.abs(speed) + jnp.sqrt(GAS * pressure * inverse)


def lift(own, own_flux, own_wave, other, direction, sign):
    inverse, speed, pressure = primitives(other, direction)
    other_flux = fluxes(other, speed, pressure, direction)
    top = jnp.maximum(own_wave, wave(inverse, speed, pressure))
    return [
        3.0 * (sign * (other_flux[v] - own_flux[v]) + top * (other[v] - own[v])) for v in range(5)
    ]


def derivative(values):
    out = []
    for i in range(4):
        row = []
        for v in range(5):
            total = None
            for j in range(4):
                if abs(D[i][j]) > 1e-12:
                    term = (-D[i][j]) * values[j][v]
                    total = term if total is None else total + term
            row.append(total)
        out.append(row)
    return out


def strided(ref, at, v, pair, c):
    return ref[at, v, pl.ds(32 * pair + c, 8, 4), :]


def rows(ref, at, v, start):
    return ref[at, v, pl.ds(start, 8), :]


def pass_z(u, at, before, after, out, to, tile):
    lane = lanes()
    base = lax.rem(48 * tile, 80)
    place = lane + base
    first = (place == 0) | (place == 80) | (place == 160)
    last = (place == 79) | (place == 159)
    for pair in range(2):
        state = [[strided(u, at, v, pair, c) for v in range(5)] for c in range(4)]
        prims = [primitives(state[c], 2) for c in range(4)]
        flux = [fluxes(state[c], prims[c][1], prims[c][2], 2) for c in range(4)]
        rate = derivative(flux)
        left = []
        right = []
        for v in range(5):
            back = strided(u, before, v, pair, 3)
            ahead = strided(u, after, v, pair, 3)
            near = turn(jnp.where(lane == 127, back, state[3][v]), 1)
            far = turn(jnp.where(lane >= 79, state[3][v], ahead), 49)
            left.append(jnp.where(first, far, near))
            back = strided(u, before, v, pair, 0)
            ahead = strided(u, after, v, pair, 0)
            near = turn(jnp.where(lane == 0, ahead, state[0][v]), 127)
            far = turn(jnp.where(lane >= 49, back, state[0][v]), 79)
            right.append(jnp.where(last, far, near))
        low = lift(state[0], flux[0], wave(*prims[0]), left, 2, 1.0)
        high = lift(state[3], flux[3], wave(*prims[3]), right, 2, -1.0)
        for v in range(5):
            for c in range(4):
                value = rate[c][v]
                if c == 0:
                    value = value + low[v]
                if c == 3:
                    value = value + high[v]
                out[to, v, pl.ds(32 * pair + c, 8, 4), :] = value


def pass_y(u, at, before, after, out, to):
    lane = lanes()
    half = upper_half()
    sign = jnp.where(half, 1.0, -1.0).astype(jnp.float32)

    def two(x, y):
        return jnp.where(half, jnp.float32(-x), jnp.float32(-y))

    mix_low = [two(D[0][0], D[1][1]), two(D[0][1], D[1][0]), two(D[0][2], D[1][3]), two(D[0][3], D[1][2])]
    mix_high = [two(D[2][0], D[3][1]), two(D[2][1], D[3][0]), two(D[2][2], D[3][3]), two(D[2][3], D[3][2])]
    for a in range(4):
        low = [rows(u, at, v, 16 * a) for v in range(5)]
        high = [rows(u, at, v, 16 * a + 8) for v in range(5)]
        prim_low = primitives(low, 1)
        prim_high = primitives(high, 1)
        flux_low = fluxes(low, prim_low[1], prim_low[2], 1)
        flux_high = fluxes(high, prim_high[1], prim_high[2], 1)
        own = [jnp.where(half, low[v], high[v]) for v in range(5)]
        own_flux = [jnp.where(half, flux_low[v], flux_high[v]) for v in range(5)]
        own_wave = wave(*[jnp.where(half, x, y) for x, y in zip(prim_low, prim_high)])
        other = []
        for v in range(5):
            back = rows(u, before, v, 16 * a + 8)
            ahead = rows(u, after, v, 16 * a)
            down = turn(jnp.where(lane >= 48, back, high[v]), 80)
            up = turn(jnp.where(lane >= 80, low[v], ahead), 48)
            other.append(swap(jnp.where(half, up, down)))
        face = lift(own, own_flux, own_wave, other, 1, sign)
        for v in range(5):
            parts = [flux_low[v], swap(flux_low[v]), flux_high[v], swap(flux_high[v])]
            sum_low = jnp.where(half, face[v], 0.0)
            sum_high = jnp.where(half, 0.0, face[v])
            for k in range(4):
                sum_low = sum_low + mix_low[k] * parts[k]
                sum_high = sum_high + mix_high[k] * parts[k]
            out[to, v, pl.ds(16 * a, 8), :] += sum_low
            out[to, v, pl.ds(16 * a + 8, 8), :] += sum_high


def pass_x(u, at, out, to):
    for h in range(2):
        state = [[rows(u, at, v, 16 * a + 8 * h) for v in range(5)] for a in range(4)]
        flux = []
        for a in range(4):
            _, speed, pressure = primitives(state[a], 0)
            flux.append(fluxes(state[a], speed, pressure, 0))
        rate = derivative(flux)
        for a in range(4):
            for v in range(5):
                out[to, v, pl.ds(16 * a + 8 * h, 8), :] += rate[a][v]


def faces_x(u, at, lower, low_at, upper, up_at, out, to):
    for h in range(2):
        for a, other, sign in ((0, lower, 1.0), (3, upper, -1.0)):
            own = [rows(u, at, v, 16 * a + 8 * h) for v in range(5)]
            inverse, speed, pressure = primitives(own, 0)
            own_flux = fluxes(own, speed, pressure, 0)
            trace = [other(v, h) for v in range(5)]
            face = lift(own, own_flux, wave(inverse, speed, pressure), trace, 0, sign)
            for v in range(5):
                out[to, v, pl.ds(16 * a + 8 * h, 8), :] += face[v]


def inner_rate(u, at, before, after, out, to, tile):
    pass_z(u, at, before, after, out, to, tile)
    pass_y(u, at, before, after, out, to)
    pass_x(u, at, out, to)


def pack(ref, at, side, tile):
    lane = lanes()
    half = upper_half()
    packed = []
    for v in range(5):
        for pair in range(2):
            if side == 0:
                one = rows(ref, at, v, 32 * pair + 8)
                two = rows(ref, at, v, 32 * pair + 24)
                main = jnp.where(half, swap(one), two)
            else:
                one = rows(ref, at, v, 32 * pair)
                two = rows(ref, at, v, 32 * pair + 16)
                main = jnp.where(half, one, swap(two))
            if tile is not None:
                c0 = strided(ref, at, v, pair, 0)
                c3 = strided(ref, at, v, pair, 3)
                if side == 0:
                    main = jnp.where(lane == 0, turn(c0, 8 + 8 * tile), main)
                    main = jnp.where(lane == 1, turn(c3, 2), main)
                else:
                    main = jnp.where(lane == 127, turn(c0, 127), main)
                    main = jnp.where(lane == 126, turn(c3, 47 + 8 * tile), main)
            packed.append(main)
    return packed


def unpack(packed, ref, at, side, columns):
    for v in range(5):
        for pair in range(2):
            block = packed[2 * v + pair]
            if columns:
                at0, at3 = (0, 1) if side == 0 else (127, 126)
                c0 = jnp.broadcast_to(block[:, at0 : at0 + 1], (8, 128))
                c3 = jnp.broadcast_to(block[:, at3 : at3 + 1], (8, 128))
                ref[at, v, pl.ds(32 * pair, 8, 4), :] = c0
                ref[at, v, pl.ds(32 * pair + 3, 8, 4), :] = c3
            shift = 12 if side == 0 else 0
            ref[at, v, pl.ds(32 * pair + shift, 4), :] = block[0:4]
            ref[at, v, pl.ds(32 * pair + 16 + shift, 4), :] = block[4:8]


def squeeze(packed, side):
    lane = lanes()
    blocks = [turn(block, 80) for block in packed] if side == 0 else packed
    full = [jnp.where(lane < 64, blocks[2 * i], turn(blocks[2 * i + 1], 64)) for i in range(5)]
    for group in (range(8), range(8, 10)):
        tail = turn(blocks[group[0]], 64)
        for g, k in enumerate(group):
            if g:
                tail = jnp.where(lane >= 16 * g, turn(blocks[k], (64 + 16 * g) % 128), tail)
        full.append(tail)
    return full


def stretch(full, side):
    lane = lanes()
    packed = []
    for k in range(10):
        main = full[k // 2]
        if k % 2:
            main = turn(main, 64)
        tail = full[5 + k // 8]
        shift = (64 - 16 * (k % 8)) % 128
        if shift:
            tail = turn(tail, shift)
        block = jnp.where(lane < 64, main, tail)
        packed.append(turn(block, 48) if side == 0 else block)
    return packed


MID_FIRST = 3
HELPER = -2
ONWARD = 1 - HELPER


def relayed(t):
    return (t == 1) | (t == 2) | (t == 3) | (t == 7) | (t == 8) | (t == 6)


def kernel(
    start_hbm,
    offset_hbm,
    out_hbm,
    start,
    u0,
    x_low,
    x_high,
    rate,
    halo_send,
    landed,
    halo,
    u1,
    x_low2,
    x_high2,
    rate2,
    give,
    pair_send,
    pair_land,
    relay,
    load_sem,
    x_send,
    x_recv,
    mid_send,
    mid_recv,
    end_send,
    end_recv,
    halo_ssem,
    halo_rsem,
    own_sem,
    own_halo_sem,
    x_send2,
    x_recv2,
    give_send,
    give_recv,
    give_own,
    pair_ssem,
    pair_rsem,
    relay_send,
    relay_recv,
    onward_send,
):
    m = lax.axis_index("node")
    s = lax.axis_index("space")
    hi = (s // 8) % 2
    q = m + hi * (3 - 2 * m)
    odd = q % 2
    left = 1 - q // 2
    up = (s + 1) % 64
    down = (s + 63) % 64
    hi_up = (up // 8) % 2
    hi_down = (down // 8) % 2
    q_up = q + hi_up * (3 - 2 * q)
    q_down = q + hi_down * (3 - 2 * q)
    slot_from = (3 - q) // 3
    slot_to = 3 - q // 3
    first_tile = 3 * q - 1
    k_from = 1 - (q % 3 + 1) // 2
    other_q = q + 1 - 2 * odd
    partner = other_q + hi * (3 - 2 * other_q)
    far_up = s % 8 == 7
    far_down = s % 8 == 0
    helps_up = s % 8 == (7 + HELPER) % 8
    helps_down = s % 8 == (-HELPER) % 8

    def space(distance):
        return (s + 64 + distance) % 64

    def turn_of(i):
        g = i % 5
        near = (g % 2) * ((g - 1) // 2) + (1 - g % 2) * (4 - g // 2)
        flip = (i // 5 + left) % 2
        return near + flip * (9 - 2 * near)

    def place_of(d):
        return d + hi * (3 - 2 * d)

    def loads(t):
        return (
            pltpu.make_async_copy(start_hbm.at[:, :, t, 0, :], start.at[t], load_sem.at[0, t]),
            pltpu.make_async_copy(offset_hbm.at[:, :, t, 0, :], u0.at[t], load_sem.at[1, t]),
        )

    def begin(i, carry):
        one, two = loads(turn_of(i))
        one.start()
        two.start()
        return carry

    lax.fori_loop(0, TILES, begin, 0)

    barrier = pltpu.get_barrier_semaphore()
    for k in range(1, 4):
        pl.semaphore_signal(barrier, inc=1, device_id={"node": (m + k) % 4}, device_id_type=MESH)
    pl.semaphore_signal(barrier, inc=1, device_id={"space": up}, device_id_type=MESH)
    pl.semaphore_signal(barrier, inc=1, device_id={"space": down}, device_id_type=MESH)
    pl.semaphore_signal(barrier, inc=1, device_id={"node": q_up, "space": up}, device_id_type=MESH)
    pl.semaphore_signal(barrier, inc=1, device_id={"node": q_down, "space": down}, device_id_type=MESH)
    for role, friends in (
        (far_up, (HELPER, 1 - HELPER)),
        (far_down, (-HELPER, HELPER - 1)),
        (helps_up, (-HELPER, ONWARD)),
        (helps_down, (HELPER, -ONWARD)),
    ):

        @pl.when(role)
        def _(friends=friends):
            for friend in friends:
                pl.semaphore_signal(
                    barrier, inc=1, device_id={"space": space(friend)}, device_id_type=MESH
                )

    in_relay = far_up | far_down | helps_up | helps_down

    @pl.when(in_relay)
    def _():
        pl.semaphore_wait(barrier, 9)

    @pl.when(jnp.logical_not(in_relay))
    def _():
        pl.semaphore_wait(barrier, 7)


    def x_copies(t):
        return (
            pltpu.make_async_remote_copy(
                src_ref=u0.at[t, :, pl.ds(48, 16)],
                dst_ref=x_low.at[t],
                send_sem=x_send.at[0, t],
                recv_sem=x_recv.at[0, t],
                device_id={"space": up},
                device_id_type=MESH,
            ),
            pltpu.make_async_remote_copy(
                src_ref=u0.at[t, :, pl.ds(0, 16)],
                dst_ref=x_high.at[t],
                send_sem=x_send.at[1, t],
                recv_sem=x_recv.at[1, t],
                device_id={"space": down},
                device_id_type=MESH,
            ),
        )

    def relay_copies(t):
        return (
            pltpu.make_async_remote_copy(
                src_ref=u0.at[t, :, pl.ds(48, 16)],
                dst_ref=relay.at[t],
                send_sem=relay_send.at[t],
                recv_sem=relay_recv.at[t],
                device_id={"space": space(HELPER)},
                device_id_type=MESH,
            ),
            pltpu.make_async_remote_copy(
                src_ref=u0.at[t, :, pl.ds(0, 16)],
                dst_ref=relay.at[t],
                send_sem=relay_send.at[t],
                recv_sem=relay_recv.at[t],
                device_id={"space": space(-HELPER)},
                device_id_type=MESH,
            ),
        )

    def onward_copies(t):
        return (
            pltpu.make_async_remote_copy(
                src_ref=relay.at[t],
                dst_ref=x_low.at[t],
                send_sem=onward_send.at[t],
                recv_sem=x_recv.at[0, t],
                device_id={"space": space(ONWARD)},
                device_id_type=MESH,
            ),
            pltpu.make_async_remote_copy(
                src_ref=relay.at[t],
                dst_ref=x_high.at[t],
                send_sem=onward_send.at[t],
                recv_sem=x_recv.at[1, t],
                device_id={"space": space(-ONWARD)},
                device_id_type=MESH,
            ),
        )

    def guess(i, carry):
        t = turn_of(i)
        one, two = loads(t)
        one.wait()
        two.wait()
        for v in range(5):
            u0[t, v] = u0[t, v] + start[t, v]
        one, two = x_copies(t)
        by_up, by_down = relay_copies(t)

        @pl.when(far_up & relayed(t))
        def _():
            by_up.start()

        @pl.when(jnp.logical_not(far_up & relayed(t)))
        def _():
            one.start()

        @pl.when(far_down & relayed(t))
        def _():
            by_down.start()

        @pl.when(jnp.logical_not(far_down & relayed(t)))
        def _():
            two.start()

        return carry

    lax.fori_loop(0, TILES, guess, 0)

    def owner(t):
        return (t + 1) // 3

    def mid_copy(t):
        d = owner(t)
        slot = t - 3 * d + 1
        return pltpu.make_async_remote_copy(
            src_ref=rate.at[t, :, pl.ds(16, 32)],
            dst_ref=landed.at[m, slot, :, pl.ds(16, 32)],
            send_sem=mid_send.at[t],
            recv_sem=mid_recv.at[m, slot],
            device_id={"node": place_of(d)},
            device_id_type=MESH,
        )

    def end_copies(t):
        d = owner(t)
        slot = t - 3 * d + 1
        return [
            pltpu.make_async_remote_copy(
                src_ref=rate.at[t, :, pl.ds(48 * k, 16)],
                dst_ref=landed.at[m, slot, :, pl.ds(48 * k, 16)],
                send_sem=end_send.at[k, t],
                recv_sem=end_recv.at[k, m, slot],
                device_id={"node": place_of(d)},
                device_id_type=MESH,
            )
            for k in range(2)
        ]

    def own_copy(slot):
        return pltpu.make_async_copy(
            rate.at[first_tile + slot], landed.at[m, slot], own_sem.at[slot]
        )

    def send_mid(i):
        t = turn_of(i)

        @pl.when(owner(t) != q)
        def _():
            mid_copy(t).start()

    def onward(t, carry):
        one, two = onward_copies(t)

        @pl.when(helps_up & relayed(t))
        def _():
            relay_copies(t)[0].wait_recv()
            one.start()

        @pl.when(helps_down & relayed(t))
        def _():
            relay_copies(t)[1].wait_recv()
            two.start()

        return carry

    def inside(i, carry):
        t = turn_of(i)
        inner_rate(u0, t, (t + 9) % 10, (t + 1) % 10, rate, t, t)

        @pl.when(i < MID_FIRST)
        def _():
            send_mid(i)

        @pl.when(i == 6)
        def _():
            lax.fori_loop(1, 9, onward, 0)

        return carry

    lax.fori_loop(0, TILES, inside, 0)


    def edges(i, carry):
        t = turn_of(i)
        one, two = x_copies(t)
        one.wait_recv()
        two.wait_recv()
        faces_x(
            u0,
            t,
            lambda v, h: x_low[t, v, pl.ds(8 * h, 8), :],
            t,
            lambda v, h: x_high[t, v, pl.ds(8 * h, 8), :],
            t,
            rate,
            t,
        )

        @pl.when(owner(t) != q)
        def _():
            for copy in end_copies(t):
                copy.start()

        @pl.when(owner(t) == q)
        def _():
            own_copy(t - first_tile).start()

        return carry

    lax.fori_loop(0, TILES, edges, 0)

    def halo_copy(d):
        return pltpu.make_async_remote_copy(
            src_ref=halo_send.at[d],
            dst_ref=halo.at[m],
            send_sem=halo_ssem.at[d],
            recv_sem=halo_rsem.at[m],
            device_id={"node": place_of(d)},
            device_id_type=MESH,
        )

    own_halo = pltpu.make_async_copy(halo_send.at[q], halo.at[m], own_halo_sem)

    for d, side, tile in ((0, 0, 9), (1, 1, 5), (2, 0, 4), (3, 1, 0)):
        for k, block in enumerate(squeeze(pack(rate, tile, side, None), side)):
            halo_send[d, pl.ds(8 * k, 8), :] = block

    def borders(d, carry):
        @pl.when(d != q)
        def _():
            halo_copy(d).start()

        return carry

    lax.fori_loop(0, 4, borders, 0)
    own_halo.start()

    def rest(i, carry):
        send_mid(i)
        return carry

    lax.fori_loop(MID_FIRST, TILES, rest, 0)

    def arrived(part, sem):
        pltpu.make_async_remote_copy(
            src_ref=part,
            dst_ref=part,
            send_sem=mid_send.at[0],
            recv_sem=sem,
            device_id={"node": (m + 1) % 4},
            device_id_type=MESH,
        ).wait_recv()

    def x_copies2(slot):
        return (
            pltpu.make_async_remote_copy(
                src_ref=u1.at[:, slot + 1, :, pl.ds(48, 16)],
                dst_ref=x_low2.at[slot],
                send_sem=x_send2.at[0, slot],
                recv_sem=x_recv2.at[0, slot],
                device_id={"node": q_up, "space": up},
                device_id_type=MESH,
            ),
            pltpu.make_async_remote_copy(
                src_ref=u1.at[:, slot + 1, :, pl.ds(0, 16)],
                dst_ref=x_high2.at[slot],
                send_sem=x_send2.at[1, slot],
                recv_sem=x_recv2.at[1, slot],
                device_id={"node": q_down, "space": down},
                device_id_type=MESH,
            ),
        )

    def advance(slot, offset, stride):
        def each(v, inner):
            for part in range(4):
                at = offset + 8 * (part % 2) + stride * (part // 2)
                held = [landed[j, slot, v, pl.ds(at, 8), :] for j in range(4)]
                base = start[first_tile + slot, v, pl.ds(at, 8), :]
                for k in range(4):
                    total = Q[k][0] * held[0]
                    for j in range(1, 4):
                        total = total + Q[k][j] * held[j]
                    u1[k, slot + 1, v, pl.ds(at, 8), :] = base + total
            return inner

        lax.fori_loop(0, 5, each, 0)

    def next_state(slot):
        def ends(j, carry):
            @pl.when(j != m)
            def _():
                for k in range(2):
                    arrived(landed.at[j, slot, :, pl.ds(48 * k, 16)], end_recv.at[k, j, slot])

            return carry

        own_copy(slot).wait()
        lax.fori_loop(0, 4, ends, 0)
        advance(slot, 0, 48)
        one, two = x_copies2(slot)
        one.start()
        two.start()

        def mids(j, carry):
            @pl.when(j != m)
            def _():
                arrived(landed.at[j, slot, :, pl.ds(16, 32)], mid_recv.at[j, slot])

            return carry

        lax.fori_loop(0, 4, mids, 0)
        advance(slot, 16, 16)

    def middle_rows():
        def wait(j, carry):
            @pl.when(j != m)
            def _():
                arrived(halo.at[j], halo_rsem.at[j])

            return carry

        own_halo.wait()
        lax.fori_loop(0, 4, wait, 0)

        def fill(side, tile, at):
            base = squeeze(pack(start, tile, side, None), side)
            held = [[halo[j, pl.ds(8 * k, 8), :] for k in range(7)] for j in range(4)]
            for node in range(4):
                blocks = []
                for k in range(7):
                    total = Q[node][0] * held[0][k]
                    for j in range(1, 4):
                        total = total + Q[node][j] * held[j][k]
                    blocks.append(base[k] + total)
                unpack(stretch(blocks, side), u1.at[node], at, side, False)

        @pl.when(odd == 0)
        def _():
            fill(0, (first_tile + slot_from + 9) % 10, slot_from)

        @pl.when(odd == 1)
        def _():
            fill(1, (first_tile + slot_to) % 10, slot_to + 1)

    pair_copy = pltpu.make_async_remote_copy(
        src_ref=pair_send,
        dst_ref=pair_land,
        send_sem=pair_ssem,
        recv_sem=pair_rsem,
        device_id={"node": partner},
        device_id_type=MESH,
    )

    def pair_out(slot):
        def give_rows(side):
            def each(node, carry):
                blocks = pack(u1.at[node], slot + 1, side, first_tile + slot)
                for k, block in enumerate(blocks):
                    pair_send[node, pl.ds(8 * k, 8), :] = block
                return carry

            lax.fori_loop(0, 4, each, 0)

        @pl.when(odd == 0)
        def _():
            give_rows(0)

        @pl.when(odd == 1)
        def _():
            give_rows(1)

        pair_copy.start()

    def pair_in():
        pair_copy.wait_recv()

        def take_rows(side, at):
            def each(node, carry):
                blocks = [pair_land[node, pl.ds(8 * k, 8), :] for k in range(10)]
                unpack(blocks, u1.at[node], at, side, True)
                return carry

            lax.fori_loop(0, 4, each, 0)

        @pl.when(odd == 0)
        def _():
            take_rows(1, slot_to + 1)

        @pl.when(odd == 1)
        def _():
            take_rows(0, slot_from)

    def give_copy(node, slot):
        return pltpu.make_async_remote_copy(
            src_ref=give.at[node, slot],
            dst_ref=out_hbm.at[:, :, first_tile + slot, 0, :],
            send_sem=give_send.at[node, slot],
            recv_sem=give_recv.at[first_tile + slot],
            device_id={"node": node},
            device_id_type=MESH,
        )

    def give_here(slot):
        return pltpu.make_async_copy(
            give.at[m, slot], out_hbm.at[:, :, first_tile + slot, 0, :], give_own.at[slot]
        )

    def second(slot):
        def each(node, carry):
            inner_rate(
                u1.at[node], slot + 1, slot, slot + 2, rate2.at[node], slot, first_tile + slot
            )
            return carry

        lax.fori_loop(0, 4, each, 0)
        one, two = x_copies2(slot)
        one.wait_recv()
        two.wait_recv()

        def edge(node, carry):
            faces_x(
                u1.at[node],
                slot + 1,
                lambda v, h: x_low2[slot, node, v, pl.ds(8 * h, 8), :],
                slot,
                lambda v, h: x_high2[slot, node, v, pl.ds(8 * h, 8), :],
                slot,
                rate2.at[node],
                slot,
            )
            return carry

        lax.fori_loop(0, 4, edge, 0)

        def gather(v, carry):
            for part in range(8):
                held = [rate2[j, slot, v, pl.ds(8 * part, 8), :] for j in range(4)]
                for k in range(4):
                    total = Q[k][0] * held[0]
                    for j in range(1, 4):
                        total = total + Q[k][j] * held[j]
                    give[k, slot, v, pl.ds(8 * part, 8), :] = total
            return carry

        lax.fori_loop(0, 5, gather, 0)

        def send(k, carry):
            node = (3 - k) * (1 - m // 2) + k * (m // 2)

            @pl.when(node != m)
            def _():
                give_copy(node, slot).start()

            @pl.when(node == m)
            def _():
                give_here(slot).start()

            return carry

        lax.fori_loop(0, 4, send, 0)

    def slot_of(k):
        return k + odd * (2 - 2 * k)

    def stage(k, carry):
        @pl.when(k < 3)
        def _():
            next_state(slot_of(k))

        @pl.when(k == 2)
        def _():
            pair_out(slot_of(k))

        @pl.when(k == k_from + 1)
        def _():
            middle_rows()

        @pl.when(k == 3)
        def _():
            pair_in()

        @pl.when(k > k_from)
        def _():
            second(slot_of(k - 1))

        return carry

    lax.fori_loop(k_from, 4, stage, 0)

    def drain(t, carry):
        one, two = x_copies(t)
        by_up, by_down = relay_copies(t)
        on_up, on_down = onward_copies(t)

        @pl.when(far_up & relayed(t))
        def _():
            by_up.wait_send()

        @pl.when(jnp.logical_not(far_up & relayed(t)))
        def _():
            one.wait_send()

        @pl.when(far_down & relayed(t))
        def _():
            by_down.wait_send()

        @pl.when(jnp.logical_not(far_down & relayed(t)))
        def _():
            two.wait_send()

        @pl.when(helps_up & relayed(t))
        def _():
            on_up.wait_send()

        @pl.when(helps_down & relayed(t))
        def _():
            on_down.wait_send()

        @pl.when(owner(t) != q)
        def _():
            mid_copy(t).wait_send()
            for copy in end_copies(t):
                copy.wait_send()
            arrived(out_hbm.at[:, :, t, 0, :], give_recv.at[t])

        return carry

    lax.fori_loop(0, TILES, drain, 0)

    def drain_nodes(d, carry):
        @pl.when(d != q)
        def _():
            halo_copy(d).wait_send()

        return carry

    lax.fori_loop(0, 4, drain_nodes, 0)
    pair_copy.wait_send()

    def drain_slots(slot, carry):
        one, two = x_copies2(slot)
        one.wait_send()
        two.wait_send()
        give_here(slot).wait()

        def each(node, inner):
            @pl.when(node != m)
            def _():
                give_copy(node, slot).wait_send()

            return inner

        lax.fori_loop(0, 4, each, 0)
        return carry

    lax.fori_loop(slot_from, slot_to, drain_slots, 0)


def body(start_state, node_offset):
    flat = (5, 64, TILES, 1, 128)
    vmem = lambda *shape: pltpu.VMEM(shape, jnp.float32)
    dma = lambda *shape: pltpu.SemaphoreType.DMA(shape)
    out = pl.pallas_call(
        kernel,
        out_shape=jax.ShapeDtypeStruct(flat, jnp.float32),
        in_specs=[pl.BlockSpec(memory_space=pltpu.HBM)] * 2,
        out_specs=pl.BlockSpec(memory_space=pl.ANY),
        scratch_shapes=[
            vmem(10, 5, 64, 128),
            vmem(10, 5, 64, 128),
            vmem(10, 5, 16, 128),
            vmem(10, 5, 16, 128),
            vmem(10, 5, 64, 128),
            vmem(4, 56, 128),
            vmem(4, 3, 5, 64, 128),
            vmem(4, 56, 128),
            vmem(4, 5, 5, 64, 128),
            vmem(3, 4, 5, 16, 128),
            vmem(3, 4, 5, 16, 128),
            vmem(4, 3, 5, 64, 128),
            vmem(4, 3, 5, 64, 128),
            vmem(4, 80, 128),
            vmem(4, 80, 128),
            vmem(10, 5, 16, 128),
            dma(2, 10),
            dma(2, 10),
            dma(2, 10),
            dma(10),
            dma(4, 3),
            dma(2, 10),
            dma(2, 4, 3),
            dma(4),
            dma(4),
            dma(3),
            pltpu.SemaphoreType.DMA,
            dma(2, 3),
            dma(2, 3),
            dma(4, 3),
            dma(10),
            dma(3),
            pltpu.SemaphoreType.DMA,
            pltpu.SemaphoreType.DMA,
            dma(10),
            dma(10),
            dma(10),
        ],
        compiler_params=pltpu.CompilerParams(
            collective_id=0, has_side_effects=True, vmem_limit_bytes=52 << 20
        ),
    )(start_state.reshape(flat), node_offset.reshape(flat))
    return out.reshape((1,) + start_state.shape)


def solution(mesh):
    return jax.shard_map(
        body,
        mesh=mesh,
        in_specs=(
            P(None, None, None, None, "space", None),
            P("node", None, None, None, None, "space", None),
        ),
        out_specs=P("node", None, None, None, None, "space", None),
        check_vma=False,
    )
```
